512 devices in a mesh: seq: 128 (over x, y_hi, z, core), tp: 4 (over y_lo).
Axes of the slice: x: 4, y: 8 (y_hi: 2, y_lo: 4; y = y_hi * 4 + y_lo), z: 8, core: 2. Of those that a mesh axis runs over, the one named last changes fastest.
Arguments:
- tokens: bfloat16 [16384, 2560], P('seq', 'tp'), may hold values from -6 to 6
- seg_ids: int32 [16384], P('seq'), may hold values from 0 to 31, never falling along the last dimension, each value on 1 to 4096 neighbouring positions
- norm_gain: bfloat16 [2560], replicated, may hold values from 0.099609375 to 1.8984375
- w_query: bfloat16 [2560, 2048], P('seq', 'tp'), may hold values from -3 to 3
- w_keyval: bfloat16 [2560, 512], P('seq'), may hold values from -1 to 1
- w_out: bfloat16 [2048, 2560], P('tp', 'seq'), may hold values from -0.125 to 0.125
Outputs:
- hidden: bfloat16 [16384, 2560], P('seq', 'tp')
- kv_cache: bfloat16 [16384, 512], P('seq')
The draws below stay inside these ranges and needn't reach their ends.
Inputs may be any that keep to these rules, and one draw needn't show every extreme that they name: `seg_ids`: ids never fall along the stream; each of the 32 requests holds 1 to 4096 consecutive tokens, one exactly 4096.
All inputs are finite; a program needn't handle non-finite values.
Results may differ from the reference program's by a relative error of at most 0.0085.
Values may be sent and summed in bfloat16 or wider, within the bound.
No kernel may reach another device: no remote copies, remote signals or barrier semaphores. Data moves between devices by JAX's collectives and lax.ppermute only.
A program may use at most 64 MiB of HBM per device.

```python
import math
import jax
import jax.numpy as jnp
import numpy as np
from jax import lax

D = 2560
HEADS = 8
HD = 256
WINDOW = 2048
TOK_DEV = 128
TOKENS = 16384
SEGS = 32
MOST = 4096
N_TP = 4


def weight_pair(key):
    base = jax.random.fold_in(key, 7)
    key_kv = jax.random.fold_in(base, 1)
    key_query = jax.random.fold_in(base, 2)
    scale = D ** (-0.5)
    keyval = jnp.clip(jax.random.normal(key_kv, (D, 2 * HD), jnp.float32), -6.0, 6.0) * scale
    query = jnp.clip(jax.random.normal(key_query, (D, HEADS * HD), jnp.float32), -6.0, 6.0) * scale
    return (query, keyval)


def draw_w_query(key, part):
    return weight_pair(key)[0].astype(jnp.bfloat16)


def draw_w_keyval(key, part):
    return weight_pair(key)[1].astype(jnp.bfloat16)


def draw_tokens(key, part):
    values = jnp.clip(jax.random.normal(key, (TOKENS, D), jnp.float32), -6.0, 6.0)
    return values.astype(jnp.bfloat16)


def levels(stream_key, extent, cuts, least, top_value):
    level, own = 1.0, jax.random.fold_in(stream_key, 6)
    for position, shards_of in cuts:
        heights = jnp.exp(jax.random.uniform(jax.random.fold_in(own, position), (shards_of,), jnp.float32, least / len(cuts), top_value / len(cuts)))
        level = level * jnp.repeat(heights, extent[position] // shards_of).reshape([-1 if axis == position else 1 for axis in range(len(extent))])
    return level


def length_profile(amount, total, most, skew):
    weights = [(1 << 20) // math.isqrt(rank ** skew) + 1 for rank in range(2, amount + 1)]
    surplus, holding = total - most - (amount - 1), [1] * (amount - 1)
    while surplus > 0:
        free = [i for i in range(amount - 1) if holding[i] < most]
        whole, left = sum([weights[i] for i in free]), surplus
        for i in free:
            more = min(most - holding[i], max(1, left * weights[i] // whole), surplus)
            holding[i] = holding[i] + more
            surplus = surplus - more
    return np.array([most] + holding)


def uneven(key, count, total, bound, skew):
    if count == 2:
        one = jax.random.randint(key, (), max(1, total - bound), min(bound, total - 1) + 1)
        return jnp.stack([one, total - one])
    lengths = jnp.asarray(length_profile(count, total, bound, skew), jnp.int32)
    couples = (count - 1) // 2
    source_of, receiver = lengths[1:1 + 2 * couples:2], lengths[2:2 + 2 * couples:2]
    margin = jnp.minimum(source_of - 1, bound - receiver)
    moved = jax.random.randint(jax.random.fold_in(key, 1), (couples,), 0, 1 << 20) % (margin + 1)
    lengths = lengths.at[1:1 + 2 * couples:2].set(source_of - moved).at[2:2 + 2 * couples:2].set(receiver + moved)
    return lengths[jax.random.permutation(jax.random.fold_in(key, 2), count)]


def centred(rng, extent, scale, bound, shards=(), kind=jnp.bfloat16):
    entries = scale * jax.random.normal(rng, extent, jnp.float32)
    if shards:
        entries = entries * levels(rng, extent, shards, -0.22, 0.18)
    return jnp.clip(entries, -bound, bound).astype(kind)


def setup_inputs(seed: int = 0) -> dict:
    seeds = jax.random.split(jax.random.key(seed), 7)
    return {
        "tokens": draw_tokens(jax.random.fold_in(seeds[6], 71), 0),
        "seg_ids": jnp.searchsorted(jnp.cumsum(uneven(seeds[1], SEGS, TOKENS, MOST, 2)), jnp.arange(TOKENS), side="right").astype(jnp.int32),
        "norm_gain": jnp.clip(1.0 + 0.18 * jax.random.normal(seeds[2], (D,), jnp.float32), 0.099609375, 1.8984375).astype(jnp.bfloat16),
        "w_query": draw_w_query(jax.random.fold_in(seeds[6], 71), 0),
        "w_keyval": draw_w_keyval(jax.random.fold_in(seeds[6], 71), 0),
        "w_out": centred(seeds[5], (HEADS * HD, D), (HEADS * HD) ** -0.5, 0.125, ((0, 4), (1, 128))),
    }


def rms_norm(values, gain):
    wide = values.astype(jnp.float32)
    scaled = wide * lax.rsqrt(lax.optimization_barrier(jnp.mean(wide * wide, axis=-1, keepdims=True)) + 1e-06)
    return (scaled * gain.astype(jnp.float32)).astype(jnp.bfloat16)

def rotate(tensor, positions):
    quarter = tensor.shape[-1] // 4
    freq = 10000.0 ** (-jnp.arange(quarter, dtype=jnp.float32) / quarter)
    angle = positions[:, None, None] * freq
    cosine = jnp.cos(angle)
    sine = jnp.sin(angle)
    first = tensor[..., :quarter]
    second = tensor[..., quarter:2 * quarter]
    return jnp.concatenate([first * cosine - second * sine, second * cosine + first * sine, tensor[..., 2 * quarter:]], axis=-1)

def reference(tokens, seg_ids, norm_gain, w_query, w_keyval, w_out):
    normed = rms_norm(tokens, norm_gain)
    labels = jnp.arange(SEGS, dtype=jnp.int32)
    starts = lax.optimization_barrier(jnp.sum((seg_ids[None, :] < labels[:, None]).astype(jnp.int32), axis=1))
    token_index = jnp.arange(TOKENS, dtype=jnp.int32)
    own_start = jnp.take(starts, seg_ids)
    positions = (token_index - own_start).astype(jnp.float32)
    query_raw = jnp.dot(normed, w_query, preferred_element_type=jnp.float32)
    keyval_raw = jnp.dot(normed, w_keyval, preferred_element_type=jnp.float32)
    queries = rotate(query_raw.reshape(TOKENS, HEADS, HD), positions).astype(jnp.bfloat16)
    key_rows = rotate(keyval_raw[:, None, :HD], positions)[:, 0, :]
    kv_cache = jnp.concatenate([key_rows, keyval_raw[:, HD:]], axis=1).astype(jnp.bfloat16)
    pad_kv = jnp.concatenate([jnp.zeros((WINDOW, 2 * HD), jnp.bfloat16), kv_cache], axis=0)
    pad_seg = jnp.concatenate([jnp.full((WINDOW,), -1, jnp.int32), seg_ids], axis=0)

    def attend(block_idx):
        begin_at = (block_idx * TOK_DEV).astype(jnp.int32)
        q_block = lax.dynamic_slice_in_dim(queries, begin_at, TOK_DEV, 0).astype(jnp.float32)
        kv_block = lax.dynamic_slice_in_dim(pad_kv, begin_at, TOK_DEV + WINDOW, 0)
        seg_block = lax.dynamic_slice_in_dim(pad_seg, begin_at, TOK_DEV + WINDOW, 0)
        q_seg = lax.dynamic_slice_in_dim(seg_ids, begin_at, TOK_DEV, 0)
        q_index = begin_at + jnp.arange(TOK_DEV, dtype=jnp.int32)
        k_index = begin_at - WINDOW + jnp.arange(TOK_DEV + WINDOW, dtype=jnp.int32)
        live = (seg_block[None, :] == q_seg[:, None]) & (k_index[None, :] <= q_index[:, None]) & (q_index[:, None] - k_index[None, :] < WINDOW)
        scores = jnp.einsum('qhd,kd->hqk', q_block, kv_block[:, :HD].astype(jnp.float32)) * HD ** (-0.5)
        scores = jnp.where(live[None], scores, -1e+30)
        peak = lax.optimization_barrier(jnp.max(scores, axis=2, keepdims=True))
        powered = jnp.exp(scores - peak)
        weights = (powered / lax.optimization_barrier(jnp.sum(powered, axis=2, keepdims=True))).astype(jnp.bfloat16)
        result = jnp.einsum('hqk,kd->qhd', weights.astype(jnp.float32), kv_block[:, HD:].astype(jnp.float32)).astype(jnp.bfloat16)
        return result.reshape(TOK_DEV, HEADS * HD)
    attended = lax.map(attend, jnp.arange(TOKENS // TOK_DEV, dtype=jnp.int32)).reshape(TOKENS, HEADS * HD)
    group = HEADS * HD // N_TP
    summed = jnp.zeros((TOKENS, D), jnp.float32)
    for group_idx in range(N_TP):
        partial_value = jnp.dot(attended[:, group_idx * group:(group_idx + 1) * group], w_out[group_idx * group:(group_idx + 1) * group], preferred_element_type=jnp.float32).astype(jnp.bfloat16)
        summed = summed + partial_value.astype(jnp.float32)
    hidden = (tokens.astype(jnp.float32) + summed).astype(jnp.bfloat16)
    return (hidden, kv_cache)
```

```python
import jax
import jax.numpy as jnp
from jax import lax
from jax.sharding import Mesh, PartitionSpec as P

HD = 256
WINDOW = 2048
SEGS = 32
GRID = (4, 2, 8, 2)
SEQ = ("x", "yh", "z", "c")


def rms_norm(values, gain):
    wide = values.astype(jnp.float32)
    scaled = wide * lax.rsqrt(jnp.mean(wide * wide, axis=-1, keepdims=True) + 1e-06)
    return (scaled * gain.astype(jnp.float32)).astype(jnp.bfloat16)


def angles(positions):
    quarter = HD // 4
    freq = 10000.0 ** (-jnp.arange(quarter, dtype=jnp.float32) / quarter)
    angle = positions[:, None] * freq
    return jnp.cos(angle), jnp.sin(angle)


def rotate(tensor, cosine, sine):
    quarter = HD // 4
    first = tensor[:, :quarter]
    second = tensor[:, quarter : 2 * quarter]
    return jnp.concatenate(
        [
            first * cosine - second * sine,
            second * cosine + first * sine,
            tensor[:, 2 * quarter :],
        ],
        axis=-1,
    )


def after(value, *others):
    return lax.optimization_barrier((value, *others))[0]


def spread(slab, axes, count):
    copies = jnp.broadcast_to(slab[None], (count, *slab.shape))
    return lax.all_to_all(copies, axes, 0, 0, tiled=True)


def natural_to_gathered(per, rows):
    nat = lax.broadcasted_iota(jnp.int32, (per, per), 0)
    gat = lax.broadcasted_iota(jnp.int32, (per, per), 1)
    half = per // 2
    core, rest = gat // half, gat % half
    source = ((rest // rows) * 2 + core) * rows + rest % rows
    return (nat == source).astype(jnp.bfloat16)


def per_device(tokens, seg_ids, norm_gain, w_query, w_keyval, w_out):
    nx, ny, nz, nc = GRID
    tok, shard = tokens.shape
    rows = w_query.shape[0]
    cols = w_query.shape[1]
    ix, iy, iz, ic = (lax.axis_index(a) for a in SEQ)
    my_block = ix * ny + iy
    my_index = (my_block * nz + iz) * nc + ic
    bf = jnp.bfloat16

    ids = jnp.pad(seg_ids.astype(bf)[None, :], ((0, 3), (0, cols - tok)))
    kv_slab = jnp.concatenate([w_keyval, ids], axis=0)
    diagonal = [(a * nx + b, b * nx + a) for a in range(nx) for b in range(nx)]
    out_rows = lax.ppermute(w_out.T, ("x", "tp"), diagonal)
    kv_near = spread(kv_slab, ("yh", "z"), ny * nz)
    seg_near = jnp.pad(kv_near[:, rows], ((0, (-ny * nz) % 16), (0, 0)))
    kv_send = jnp.concatenate([kv_near[:, :rows].reshape(ny * nz * rows, cols), seg_near], axis=0)
    kv_all = lax.all_gather(kv_send, ("x", "c"), axis=0, tiled=False)

    qo_slab = after(jnp.concatenate([w_query, out_rows], axis=0), kv_near)
    qo_near = spread(qo_slab, ("yh", "z"), ny * nz)
    part = ny * nz * rows
    qo_send = jnp.concatenate(
        [qo_near[:, :rows].reshape(part, cols), qo_near[:, rows:].reshape(part, cols)], axis=0
    )
    qo_all = lax.all_gather(qo_send, ("x", "c"), axis=0, tiled=False)

    gathered = lax.all_gather(after(tokens, qo_near), "tp", axis=1, tiled=True)
    normed = rms_norm(gathered, norm_gain)
    perm = natural_to_gathered(shard, rows)
    normed = jnp.concatenate(
        [
            jnp.dot(normed[:, g * shard : (g + 1) * shard], perm, preferred_element_type=jnp.float32).astype(bf)
            for g in range(nx)
        ],
        axis=1,
    )

    all_ids = kv_all[:, part : part + ny * nz, :tok].astype(jnp.int32)
    labels = jnp.arange(SEGS, dtype=jnp.int32)
    starts = jnp.sum((all_ids.reshape(-1)[None, :] < labels[:, None]).astype(jnp.int32), axis=1)
    own_start = jnp.sum(jnp.where(seg_ids[:, None] == labels[None, :], starts[None, :], 0), axis=1)
    token_index = my_index * tok + jnp.arange(tok, dtype=jnp.int32)
    cosine, sine = angles((token_index - own_start).astype(jnp.float32))

    keyval_raw = jnp.dot(
        normed,
        kv_all[:, :part].reshape(nx * nc * part, cols),
        preferred_element_type=jnp.float32,
    )
    kv_cache = jnp.concatenate(
        [rotate(keyval_raw[:, :HD], cosine, sine), keyval_raw[:, HD:]], axis=1
    ).astype(bf)

    block = nz * nc
    devices = nx * ny * block
    before = lax.ppermute(kv_cache, SEQ, [(i, i + block) for i in range(devices - block)])
    chips = jnp.arange(nz, dtype=jnp.int32)
    to_send = jnp.where((chips > iz)[:, None, None], kv_cache[None], before[None])
    mine = lax.all_to_all(to_send, "z", 0, 0, tiled=True)
    at_self = (chips == iz)[:, None, None] & (ic == 0)
    partner = lax.ppermute(jnp.where(at_self, kv_cache[None], mine), "c", [(0, 1), (1, 0)])
    block_of_mine = my_block - (chips >= iz).astype(jnp.int32)
    block_of_partner = my_block - jnp.where(ic == 1, chips > iz, chips >= iz).astype(jnp.int32)
    first_of_mine = ((block_of_mine * nz + chips) * nc + ic) * tok
    first_of_partner = ((block_of_partner * nz + chips) * nc + 1 - ic) * tok
    firsts = jnp.concatenate([first_of_mine, first_of_partner, my_index[None] * tok])
    key_index = (firsts[:, None] + jnp.arange(tok, dtype=jnp.int32)[None, :]).reshape(-1)
    window_kv = jnp.concatenate(
        [mine.reshape(nz * tok, 2 * HD), partner.reshape(nz * tok, 2 * HD), kv_cache], axis=0
    )

    query_raw = jnp.dot(
        normed,
        qo_all[:, :part].reshape(nx * nc * part, cols),
        preferred_element_type=jnp.float32,
    )
    live = (key_index[None, :] <= token_index[:, None]) & (key_index[None, :] >= own_start[:, None])
    live = live & (token_index[:, None] - key_index[None, :] < WINDOW)
    all_keys = window_kv[:, :HD]
    all_values = window_kv[:, HD:]
    head_outputs = []
    for head in range(cols // HD):
        queries = rotate(query_raw[:, head * HD : (head + 1) * HD], cosine, sine).astype(bf)
        scores = lax.dot_general(
            queries, all_keys, (((1,), (1,)), ((), ())), preferred_element_type=jnp.float32
        ) * HD ** (-0.5)
        scores = jnp.where(live, scores, -1e30)
        peak = jnp.max(scores, axis=1, keepdims=True)
        powered = jnp.exp(scores - peak)
        weights = (powered / jnp.sum(powered, axis=1, keepdims=True)).astype(bf)
        head_outputs.append(
            jnp.dot(weights, all_values, preferred_element_type=jnp.float32).astype(bf)
        )
    attended = jnp.concatenate(head_outputs, axis=1)

    every = lax.all_gather(attended, "tp", axis=1, tiled=True)
    out_all = qo_all[:, part:].reshape(nx, nc * part, cols)
    summed = jnp.zeros((tok, shard), jnp.float32)
    for b in range(nx):
        natural = jnp.dot(perm, out_all[b], preferred_element_type=jnp.float32).astype(bf)
        summed = summed + lax.dot_general(
            every[:, b * cols : (b + 1) * cols],
            natural,
            (((1,), (1,)), ((), ())),
            preferred_element_type=jnp.float32,
        )
    hidden = (tokens.astype(jnp.float32) + summed).astype(bf)
    return (hidden, kv_cache)


def solution(mesh):
    fine = Mesh(mesh.devices.reshape(*GRID, mesh.shape["tp"]), (*SEQ, "tp"))
    in_specs = (P(SEQ, "tp"), P(SEQ), P(), P(SEQ, "tp"), P(SEQ, None), P("tp", SEQ))
    out_specs = (P(SEQ, "tp"), P(SEQ, None))
    return jax.shard_map(
        per_device, mesh=fine, in_specs=in_specs, out_specs=out_specs, check_vma=False
    )
```

```python
import jax
import jax.numpy as jnp
from jax import lax
from jax.sharding import Mesh, PartitionSpec as P

HD = 256
WINDOW = 2048
SEGS = 32
GRID = (4, 2, 8, 2)
SEQ = ("x", "yh", "z", "c")


def rms_norm(values, gain):
    wide = values.astype(jnp.float32)
    scaled = wide * lax.rsqrt(jnp.mean(wide * wide, axis=-1, keepdims=True) + 1e-06)
    return (scaled * gain.astype(jnp.float32)).astype(jnp.bfloat16)


def angles(positions):
    quarter = HD // 4
    freq = 10000.0 ** (-jnp.arange(quarter, dtype=jnp.float32) / quarter)
    angle = positions[:, None] * freq
    return jnp.cos(angle), jnp.sin(angle)


def rotate(tensor, cosine, sine):
    quarter = HD // 4
    first = tensor[:, :quarter]
    second = tensor[:, quarter : 2 * quarter]
    return jnp.concatenate(
        [
            first * cosine - second * sine,
            second * cosine + first * sine,
            tensor[:, 2 * quarter :],
        ],
        axis=-1,
    )


def after(value, *others):
    return lax.optimization_barrier((value, *others))[0]


def spread(slab, axes, count):
    copies = jnp.broadcast_to(slab[None], (count, *slab.shape))
    return lax.all_to_all(copies, axes, 0, 0, tiled=True)


def natural_to_gathered(per, rows, ny):
    nat = lax.broadcasted_iota(jnp.int32, (per, per), 0)
    gat = lax.broadcasted_iota(jnp.int32, (per, per), 1)
    place, row = gat // rows, gat % rows
    source = ((place % ny) * (per // rows // ny) + place // ny) * rows + row
    return (nat == source).astype(jnp.bfloat16)


def per_device(tokens, seg_ids, norm_gain, w_query, w_keyval, w_out):
    nx, ny, nz, nc = GRID
    tok, shard = tokens.shape
    rows = w_query.shape[0]
    cols = w_query.shape[1]
    ix, iy, iz, ic = (lax.axis_index(a) for a in SEQ)
    my_block = ix * ny + iy
    my_index = (my_block * nz + iz) * nc + ic
    bf = jnp.bfloat16

    pairs = [((a * ny + y) * nx + b, (b * ny + 1 - y) * nx + a) for a in range(nx) for y in range(ny) for b in range(nx)]
    diagonal = [(a * nx + b, b * nx + a) for a in range(nx) for b in range(nx)]
    out_rows = w_out.T
    q_other = lax.ppermute(w_query, "yh", [(0, 1), (1, 0)])
    o_same = lax.ppermute(out_rows, ("x", "tp"), diagonal)
    o_other = lax.ppermute(out_rows, ("x", "yh", "tp"), pairs)
    low = iy == 0
    qo_send = jnp.concatenate(
        [
            jnp.where(low, w_query, q_other),
            jnp.where(low, q_other, w_query),
            jnp.where(low, o_same, o_other),
            jnp.where(low, o_other, o_same),
        ],
        axis=0,
    )
    qo_all = lax.all_gather(qo_send, ("x", "z", "c"), axis=0, tiled=False)
    part = ny * rows

    it = lax.axis_index("tp")
    shares = jnp.stack(
        [tokens] + [lax.ppermute(tokens, "tp", [(i, (i + k) % nx) for i in range(nx)]) for k in range(1, nx)]
    )
    gathered = jnp.concatenate(
        [lax.dynamic_index_in_dim(shares, (it - g) % nx, 0, keepdims=False) for g in range(nx)], axis=1
    )
    normed = rms_norm(gathered, norm_gain)

    share = 2 * HD // nx
    ids = jnp.pad(seg_ids.astype(bf)[None, :], ((0, 3), (0, 0)))
    kv_slab = jnp.concatenate([lax.dynamic_slice_in_dim(w_keyval, it * share, share, 1), ids], axis=0)
    kv_all = spread(kv_slab, SEQ, nx * ny * nz * nc)

    all_ids = kv_all[:, rows].astype(jnp.int32)
    labels = jnp.arange(SEGS, dtype=jnp.int32)
    starts = jnp.sum((all_ids.reshape(-1)[None, :] < labels[:, None]).astype(jnp.int32), axis=1)
    own_start = jnp.sum(jnp.where(seg_ids[:, None] == labels[None, :], starts[None, :], 0), axis=1)
    token_index = my_index * tok + jnp.arange(tok, dtype=jnp.int32)
    cosine, sine = angles((token_index - own_start).astype(jnp.float32))

    kv_raw = jnp.dot(
        normed, kv_all[:, :rows].reshape(nx * shard, share), preferred_element_type=jnp.float32
    )
    turned = rotate(kv_raw, cosine, sine)
    kv_share = jnp.where(it == 0, turned, kv_raw).astype(bf)
    kv_cache = lax.all_gather(kv_share, "tp", axis=1, tiled=True)

    block = nz * nc
    devices = nx * ny * block
    before = lax.ppermute(kv_cache, SEQ, [(i, i + block) for i in range(devices - block)])
    chips = jnp.arange(nz, dtype=jnp.int32)
    to_send = jnp.where((chips > iz)[:, None, None], kv_cache[None], before[None])
    mine = lax.all_to_all(to_send, "z", 0, 0, tiled=True)
    at_self = (chips == iz)[:, None, None] & (ic == 0)
    partner = lax.ppermute(jnp.where(at_self, kv_cache[None], mine), "c", [(0, 1), (1, 0)])
    block_of_mine = my_block - (chips >= iz).astype(jnp.int32)
    block_of_partner = my_block - jnp.where(ic == 1, chips > iz, chips >= iz).astype(jnp.int32)
    first_of_mine = ((block_of_mine * nz + chips) * nc + ic) * tok
    first_of_partner = ((block_of_partner * nz + chips) * nc + 1 - ic) * tok
    firsts = jnp.concatenate([first_of_mine, first_of_partner, my_index[None] * tok])
    key_index = (firsts[:, None] + jnp.arange(tok, dtype=jnp.int32)[None, :]).reshape(-1)
    window_kv = jnp.concatenate(
        [mine.reshape(nz * tok, 2 * HD), partner.reshape(nz * tok, 2 * HD), kv_cache], axis=0
    )

    perm = natural_to_gathered(shard, rows, ny)
    reordered = jnp.concatenate(
        [
            jnp.dot(normed[:, g * shard : (g + 1) * shard], perm, preferred_element_type=jnp.float32).astype(bf)
            for g in range(nx)
        ],
        axis=1,
    )
    query_raw = jnp.dot(
        reordered,
        qo_all[:, :part].reshape(nx * shard, cols),
        preferred_element_type=jnp.float32,
    )
    live = (key_index[None, :] <= token_index[:, None]) & (key_index[None, :] >= own_start[:, None])
    live = live & (token_index[:, None] - key_index[None, :] < WINDOW)
    all_keys = window_kv[:, :HD]
    all_values = window_kv[:, HD:]
    head_outputs = []
    for head in range(cols // HD):
        queries = rotate(query_raw[:, head * HD : (head + 1) * HD], cosine, sine).astype(bf)
        scores = lax.dot_general(
            queries, all_keys, (((1,), (1,)), ((), ())), preferred_element_type=jnp.float32
        ) * HD ** (-0.5)
        scores = jnp.where(live, scores, -1e30)
        peak = jnp.max(scores, axis=1, keepdims=True)
        powered = jnp.exp(scores - peak)
        weights = (powered / jnp.sum(powered, axis=1, keepdims=True)).astype(bf)
        head_outputs.append(
            jnp.dot(weights, all_values, preferred_element_type=jnp.float32).astype(bf)
        )
    attended = jnp.concatenate(head_outputs, axis=1)

    every = lax.all_gather(attended, "tp", axis=1, tiled=True)
    out_all = qo_all[:, part:].reshape(nx, shard, cols)
    summed = jnp.zeros((tok, shard), jnp.float32)
    for b in range(nx):
        natural = jnp.dot(perm, out_all[b], preferred_element_type=jnp.float32).astype(bf)
        summed = summed + lax.dot_general(
            every[:, b * cols : (b + 1) * cols],
            natural,
            (((1,), (1,)), ((), ())),
            preferred_element_type=jnp.float32,
        )
    hidden = (tokens.astype(jnp.float32) + summed).astype(bf)
    return (hidden, kv_cache)


def solution(mesh):
    fine = Mesh(mesh.devices.reshape(*GRID, mesh.shape["tp"]), (*SEQ, "tp"))
    in_specs = (P(SEQ, "tp"), P(SEQ), P(), P(SEQ, "tp"), P(SEQ, None), P("tp", SEQ))
    out_specs = (P(SEQ, "tp"), P(SEQ, None))
    return jax.shard_map(
        per_device, mesh=fine, in_specs=in_specs, out_specs=out_specs, check_vma=False
    )
```

```python
import jax
import jax.numpy as jnp
from jax import lax
from jax.sharding import Mesh, PartitionSpec as P


HD = 256
WINDOW = 2048
SEGS = 32
GRID = (4, 2, 8, 2)
SEQ = ("x", "yh", "z", "c")


def rms_norm(values, gain):
    wide = values.astype(jnp.float32)
    scaled = wide * lax.rsqrt(jnp.mean(wide * wide, axis=-1, keepdims=True) + 1e-06)
    return (scaled * gain.astype(jnp.float32)).astype(jnp.bfloat16)


def angles(positions):
    quarter = HD // 4
    freq = 10000.0 ** (-jnp.arange(quarter, dtype=jnp.float32) / quarter)
    angle = positions[:, None] * freq
    return jnp.cos(angle), jnp.sin(angle)


def rotate(tensor, cosine, sine):
    quarter = HD // 4
    first = tensor[:, :quarter]
    second = tensor[:, quarter : 2 * quarter]
    return jnp.concatenate(
        [
            first * cosine - second * sine,
            second * cosine + first * sine,
            tensor[:, 2 * quarter :],
        ],
        axis=-1,
    )


def after(value, *others):
    return lax.optimization_barrier((value, *others))[0]


def spread(slab, axes, count):
    copies = jnp.broadcast_to(slab[None], (count, *slab.shape))
    return lax.all_to_all(copies, axes, 0, 0, tiled=True)


def natural_to_gathered(per, rows, ny):
    nat = lax.broadcasted_iota(jnp.int32, (per, per), 0)
    gat = lax.broadcasted_iota(jnp.int32, (per, per), 1)
    place, row = gat // rows, gat % rows
    source = ((place % ny) * (per // rows // ny) + place // ny) * rows + row
    return (nat == source).astype(jnp.bfloat16)


def per_device(tokens, seg_ids, norm_gain, w_query, w_keyval, w_out):
    nx, ny, nz, nc = GRID
    tok, shard = tokens.shape
    rows = w_query.shape[0]
    cols = w_query.shape[1]
    ix, iy, iz, ic = (lax.axis_index(a) for a in SEQ)
    my_block = ix * ny + iy
    my_index = (my_block * nz + iz) * nc + ic
    bf = jnp.bfloat16

    qo_own = jnp.concatenate([w_query, w_out.T], axis=0)
    qo_other = lax.ppermute(qo_own, "yh", [(0, 1), (1, 0)])
    low = jnp.where(iy == 0, qo_own, qo_other)
    high = jnp.where(iy == 0, qo_other, qo_own)
    qo_send = jnp.concatenate([low[:rows], high[:rows], low[rows:], high[rows:]], axis=0)
    qo_all = lax.all_gather(qo_send, ("x", "z", "c"), axis=0, tiled=False)
    part = ny * rows

    it = lax.axis_index("tp")
    share = 2 * HD // nx
    ids = jnp.pad(seg_ids.astype(bf)[None, :], ((0, 3), (0, 0)))
    kv_slab = jnp.concatenate([lax.dynamic_slice_in_dim(w_keyval, it * share, share, 1), ids], axis=0)
    kv_all = spread(after(kv_slab, qo_send), SEQ, nx * ny * nz * nc)

    others = [lax.ppermute(tokens, "tp", [(i, (i + k) % nx) for i in range(nx)]) for k in range(1, nx)]
    shares = [tokens, *others]
    groups = []
    for g in range(nx):
        took = (it - g) % nx
        group = shares[nx - 1]
        for k in range(nx - 1):
            group = jnp.where(took == k, shares[k], group)
        groups.append(group)
    normed = rms_norm(jnp.concatenate(groups, axis=1), norm_gain)
    perm = natural_to_gathered(shard, rows, ny)
    reordered = jnp.concatenate(
        [
            jnp.dot(normed[:, g * shard : (g + 1) * shard], perm, preferred_element_type=jnp.float32).astype(bf)
            for g in range(nx)
        ],
        axis=1,
    )
    kv_all, normed, reordered, perm = lax.optimization_barrier((kv_all, normed, reordered, perm))

    all_ids = kv_all[:, rows].astype(jnp.int32)
    labels = jnp.arange(SEGS, dtype=jnp.int32)
    starts = jnp.sum((all_ids.reshape(-1)[None, :] < labels[:, None]).astype(jnp.int32), axis=1)
    own_start = jnp.sum(jnp.where(seg_ids[:, None] == labels[None, :], starts[None, :], 0), axis=1)
    token_index = my_index * tok + jnp.arange(tok, dtype=jnp.int32)
    cosine, sine = angles((token_index - own_start).astype(jnp.float32))

    kv_raw = jnp.dot(
        normed, kv_all[:, :rows].reshape(nx * shard, share), preferred_element_type=jnp.float32
    )
    turned = rotate(kv_raw, cosine, sine)
    kv_share = jnp.where(it == 0, turned, kv_raw).astype(bf)
    kv_cache = jnp.concatenate(list(spread(kv_share, "tp", nx)), axis=1)

    block = nz * nc
    devices = nx * ny * block
    before = lax.ppermute(kv_cache, SEQ, [(i, i + block) for i in range(devices - block)])
    chips = jnp.arange(nz, dtype=jnp.int32)
    to_send = jnp.where((chips > iz)[:, None, None], kv_cache[None], before[None])
    mine = lax.all_to_all(to_send, "z", 0, 0, tiled=True)
    at_self = (chips == iz)[:, None, None] & (ic == 0)
    partner = lax.ppermute(jnp.where(at_self, kv_cache[None], mine), "c", [(0, 1), (1, 0)])
    block_of_mine = my_block - (chips >= iz).astype(jnp.int32)
    block_of_partner = my_block - jnp.where(ic == 1, chips > iz, chips >= iz).astype(jnp.int32)
    first_of_mine = ((block_of_mine * nz + chips) * nc + ic) * tok
    first_of_partner = ((block_of_partner * nz + chips) * nc + 1 - ic) * tok
    firsts = jnp.concatenate([first_of_mine, first_of_partner, my_index[None] * tok])
    key_index = (firsts[:, None] + jnp.arange(tok, dtype=jnp.int32)[None, :]).reshape(-1)
    window_kv = jnp.concatenate(
        [mine.reshape(nz * tok, 2 * HD), partner.reshape(nz * tok, 2 * HD), kv_cache], axis=0
    )

    query_raw = jnp.dot(
        reordered,
        qo_all[:, :part].reshape(nx * shard, cols),
        preferred_element_type=jnp.float32,
    )
    heads = [
        rotate(query_raw[:, h * HD : (h + 1) * HD], cosine, sine).astype(bf) for h in range(cols // HD)
    ]
    live = (key_index[None, :] <= token_index[:, None]) & (key_index[None, :] >= own_start[:, None])
    live = live & (token_index[:, None] - key_index[None, :] < WINDOW)
    all_keys = window_kv[:, :HD]
    all_values = window_kv[:, HD:]
    head_outputs = []
    for queries in heads:
        scores = lax.dot_general(
            queries, all_keys, (((1,), (1,)), ((), ())), preferred_element_type=jnp.float32
        ) * HD ** (-0.5)
        scores = jnp.where(live, scores, -1e30)
        peak = jnp.max(scores, axis=1, keepdims=True)
        powered = jnp.exp(scores - peak)
        weights = (powered / jnp.sum(powered, axis=1, keepdims=True)).astype(bf)
        head_outputs.append(
            jnp.dot(weights, all_values, preferred_element_type=jnp.float32).astype(bf)
        )
    attended = jnp.concatenate(head_outputs, axis=1)

    partial = lax.dot_general(
        attended,
        qo_all[:, part:].reshape(nx * shard, cols),
        (((1,), (1,)), ((), ())),
        preferred_element_type=jnp.float32,
    ).astype(bf)
    pieces = jnp.stack([partial[:, g * shard : (g + 1) * shard] for g in range(nx)])
    received = lax.all_to_all(pieces, "tp", 0, 0, tiled=True)
    summed = jnp.zeros((tok, shard), jnp.float32)
    for g in range(nx):
        summed = summed + lax.dot_general(
            received[g], perm, (((1,), (1,)), ((), ())), preferred_element_type=jnp.float32
        )
    hidden = (tokens.astype(jnp.float32) + summed).astype(bf)
    return (hidden, kv_cache)


def solution(mesh):
    fine = Mesh(mesh.devices.reshape(*GRID, mesh.shape["tp"]), (*SEQ, "tp"))
    in_specs = (P(SEQ, "tp"), P(SEQ), P(), P(SEQ, "tp"), P(SEQ, None), P("tp", SEQ))
    out_specs = (P(SEQ, "tp"), P(SEQ, None))
    return jax.shard_map(per_device, mesh=fine, in_specs=in_specs, out_specs=out_specs, check_vma=False)
```

```python
import jax
import jax.numpy as jnp
from jax import lax
from jax.experimental import pallas as pl
from jax.experimental.pallas import tpu as pltpu
from jax.sharding import Mesh, PartitionSpec as P


HD = 256
WINDOW = 2048
SEGS = 32
GRID = (4, 2, 8, 2)
SEQ = ("x", "yh", "z", "c")


def rms_norm(values, gain):
    wide = values.astype(jnp.float32)
    scaled = wide * lax.rsqrt(jnp.mean(wide * wide, axis=-1, keepdims=True) + 1e-06)
    return (scaled * gain.astype(jnp.float32)).astype(jnp.bfloat16)


def angles(positions):
    quarter = HD // 4
    freq = 10000.0 ** (-jnp.arange(quarter, dtype=jnp.float32) / quarter)
    angle = positions[:, None] * freq
    cosine, sine = jnp.cos(angle), jnp.sin(angle)
    return jnp.concatenate([cosine, cosine], axis=1), jnp.concatenate([-sine, sine], axis=1)


def after(value, *others):
    return lax.optimization_barrier((value, *others))[0]


def spread(slab, axes, count):
    copies = jnp.broadcast_to(slab[None], (count, *slab.shape))
    return lax.all_to_all(copies, axes, 0, 0, tiled=True)


def natural_to_gathered(per, rows, ny, nz):
    nat = lax.broadcasted_iota(jnp.int32, (per, per), 0)
    gat = lax.broadcasted_iota(jnp.int32, (per, per), 1)
    half = per // 2
    core, rest = gat // half, gat % half
    place, row = rest // rows, rest % rows
    source = (((place % ny) * nz + place // ny) * 2 + core) * rows + row
    return (nat == source).astype(jnp.bfloat16)


def queries_kernel(normed_ref, cosine_ref, sine_ref, qo_ref, out_ref, weights_ref, sem):
    groups, part, cols = weights_ref.shape
    copy = pltpu.make_async_copy(qo_ref.at[:, pl.ds(0, part), :], weights_ref, sem)
    copy.start()
    copy.wait()
    raw = jnp.dot(normed_ref[0], weights_ref[0], preferred_element_type=jnp.float32)
    for g in range(1, groups):
        raw = raw + jnp.dot(normed_ref[g], weights_ref[g], preferred_element_type=jnp.float32)
    half = HD // 2
    for h in range(cols // HD):
        lo = raw[:, h * HD : h * HD + half]
        turned = lo * cosine_ref[...] + pltpu.roll(lo, half // 2, 1) * sine_ref[...]
        out_ref[:, h * HD : h * HD + half] = turned.astype(out_ref.dtype)
        out_ref[:, h * HD + half : (h + 1) * HD] = raw[:, h * HD + half : (h + 1) * HD].astype(
            out_ref.dtype
        )


def attend_kernel(
    queries_ref, mine_ref, partner_ref, keys_at_ref, token_ref, start_ref, qo_ref, out_ref, weights_ref, sem
):
    groups, part, cols = weights_ref.shape
    copy = pltpu.make_async_copy(qo_ref.at[:, pl.ds(part, part), :], weights_ref, sem)
    copy.start()
    flat = lambda ref, t: ref[t].reshape(ref.shape[1] * ref.shape[2], ref.shape[3])
    whole = lambda t: jnp.concatenate([flat(mine_ref, t), flat(partner_ref, t)], axis=0)
    keys = jnp.concatenate([whole(0), whole(1)], axis=1)
    values = jnp.concatenate([whole(2), whole(3)], axis=1)
    at = keys_at_ref[...]
    token = token_ref[...]
    live = (at <= token) & (at >= start_ref[...]) & (token - at < WINDOW)
    heads = []
    for h in range(cols // HD):
        scores = lax.dot_general(
            queries_ref[:, h * HD : (h + 1) * HD],
            keys,
            (((1,), (1,)), ((), ())),
            preferred_element_type=jnp.float32,
        ) * HD ** (-0.5)
        scores = jnp.where(live, scores, -1e30)
        powered = jnp.exp(scores - jnp.max(scores, axis=1, keepdims=True))
        weights = (powered / jnp.sum(powered, axis=1, keepdims=True)).astype(jnp.bfloat16)
        heads.append(
            jnp.dot(weights, values, preferred_element_type=jnp.float32).astype(jnp.bfloat16)
        )
    attended = jnp.concatenate(heads, axis=1)
    copy.wait()
    for g in range(groups // 2):
        rows = jnp.concatenate([weights_ref[2 * g], weights_ref[2 * g + 1]], axis=0)
        out_ref[g] = lax.dot_general(
            attended, rows, (((1,), (1,)), ((), ())), preferred_element_type=jnp.float32
        ).astype(out_ref.dtype)


def per_device(tokens, seg_ids, norm_gain, w_query, w_keyval, w_out):
    nx, ny, nz, nc = GRID
    tok, shard = tokens.shape
    rows = w_query.shape[0]
    cols = w_query.shape[1]
    ix, iy, iz, ic = (lax.axis_index(a) for a in SEQ)
    it = lax.axis_index("tp")
    my_block = ix * ny + iy
    my_index = (my_block * nz + iz) * nc + ic
    bf = jnp.bfloat16
    both = [(0, 1), (1, 0)]

    share = 2 * HD // nx
    ids = jnp.pad(seg_ids.astype(bf)[None, :], ((0, 3), (0, 0)))
    kv_own = jnp.concatenate([lax.dynamic_slice_in_dim(w_keyval, it * share, share, 1), ids], axis=0)
    own = jnp.concatenate([w_query, w_out.T, jnp.pad(kv_own, ((0, 0), (0, cols - share)))], axis=0)
    other = lax.ppermute(own, "yh", both)
    low = jnp.where(iy == 0, own, other)
    high = jnp.where(iy == 0, other, own)

    others = [lax.ppermute(tokens, "tp", [(i, (i + k) % nx) for i in range(nx)]) for k in range(1, nx)]

    w_at, id_at = slice(2 * rows, 3 * rows), slice(3 * rows, 3 * rows + 1)
    kv_pair = jnp.concatenate([low[w_at], high[w_at], low[id_at], high[id_at]], axis=0)[:, :share]
    kv_pair = jnp.pad(kv_pair, ((0, -kv_pair.shape[0] % 8), (0, 0)))
    kv_core = spread(kv_pair, ("x", "z"), nx * nz)
    kv_twin = lax.ppermute(kv_core, "c", both)

    qo_pair = jnp.concatenate([low[:rows], high[:rows], low[rows : 2 * rows], high[rows : 2 * rows]], axis=0)
    qo_near = spread(after(qo_pair, kv_core), "z", nz)
    part = nz * ny * rows
    qo_send = jnp.concatenate(
        [
            qo_near[:, : ny * rows].reshape(part, cols),
            qo_near[:, ny * rows :].reshape(part, cols),
        ],
        axis=0,
    )
    qo_all = lax.all_gather(qo_send, ("x", "c"), axis=0, tiled=False)

    shares = [tokens, *others]
    groups = []
    for g in range(nx):
        took = (it - g) % nx
        group = shares[nx - 1]
        for k in range(nx - 1):
            group = jnp.where(took == k, shares[k], group)
        groups.append(group)
    normed = rms_norm(jnp.concatenate(groups, axis=1), norm_gain)
    perm = natural_to_gathered(shard, rows, ny, nz)
    reordered = jnp.concatenate(
        [
            jnp.dot(normed[:, g * shard : (g + 1) * shard], perm, preferred_element_type=jnp.float32).astype(bf)
            for g in range(nx)
        ],
        axis=1,
    )
    blocks = jnp.stack([reordered[:, i * part : (i + 1) * part] for i in range(nx * nc)])
    kv_core, reordered, blocks, perm = lax.optimization_barrier((kv_core, reordered, blocks, perm))

    kv_zero = jnp.where(ic == 0, kv_core, kv_twin)
    kv_one = jnp.where(ic == 0, kv_twin, kv_core)
    all_ids = jnp.concatenate(
        [kv[:, ny * rows : ny * rows + ny] for kv in (kv_core, kv_twin)], axis=0
    ).astype(jnp.int32)
    labels = jnp.arange(SEGS, dtype=jnp.int32)
    starts = jnp.sum((all_ids.reshape(-1)[None, :] < labels[:, None]).astype(jnp.int32), axis=1)
    own_start = jnp.sum(jnp.where(seg_ids[:, None] == labels[None, :], starts[None, :], 0), axis=1)
    token_index = my_index * tok + jnp.arange(tok, dtype=jnp.int32)
    cosine, sine = angles((token_index - own_start).astype(jnp.float32))

    kv_rows = jnp.stack(
        [
            kv[:, : ny * rows].reshape(nx, part, share)
            for kv in (kv_zero, kv_one)
        ],
        axis=1,
    ).reshape(nx * nc * part, share)
    kv_raw = jnp.dot(reordered, kv_rows, preferred_element_type=jnp.float32)
    quarter = HD // 4
    swapped = jnp.concatenate([kv_raw[:, quarter:], kv_raw[:, :quarter]], axis=1)
    kv_share = jnp.where(it == 0, kv_raw * cosine + swapped * sine, kv_raw).astype(bf)

    block = nz * nc
    devices = nx * ny * block
    before = lax.ppermute(kv_share, SEQ, [(i, i + block) for i in range(devices - block)])
    chips = jnp.arange(nz, dtype=jnp.int32)
    to_send = jnp.where((chips > iz)[:, None, None], kv_share[None], before[None])
    near = lax.all_to_all(after(to_send, qo_send), "z", 0, 0, tiled=True)
    mine = spread(jnp.concatenate([near, kv_share[None]], axis=0), "tp", nx)
    kv_cache = jnp.concatenate([mine[t, nz] for t in range(nx)], axis=1)
    at_self = (chips == iz)[None, :, None, None] & (ic == 0)
    partner = lax.ppermute(jnp.where(at_self, mine[:, nz:], mine[:, :nz]), "c", both)
    block_of_mine = my_block - (chips >= iz).astype(jnp.int32)
    block_of_partner = my_block - jnp.where(ic == 1, chips > iz, chips >= iz).astype(jnp.int32)
    first_of_mine = ((block_of_mine * nz + chips) * nc + ic) * tok
    first_of_partner = ((block_of_partner * nz + chips) * nc + 1 - ic) * tok
    firsts = jnp.concatenate([first_of_mine, my_index[None] * tok, first_of_partner])
    keys_at = (firsts[:, None] + jnp.arange(tok, dtype=jnp.int32)[None, :]).reshape(1, -1)

    vmem = pl.BlockSpec(memory_space=pltpu.VMEM)
    hbm = pl.BlockSpec(memory_space=pl.ANY)
    scratch = [pltpu.VMEM((nx * nc, part, cols), bf), pltpu.SemaphoreType.DMA]
    queries = pl.pallas_call(
        queries_kernel,
        out_shape=jax.ShapeDtypeStruct((tok, cols), bf),
        in_specs=[vmem, vmem, vmem, hbm],
        out_specs=vmem,
        scratch_shapes=scratch,
        name="queries",
    )(blocks, cosine, sine, qo_all)
    partial = pl.pallas_call(
        attend_kernel,
        out_shape=jax.ShapeDtypeStruct((nx, tok, shard), bf),
        in_specs=[vmem] * 6 + [hbm],
        out_specs=vmem,
        scratch_shapes=scratch,
        name="attend",
    )(queries, mine, partner, keys_at, token_index[:, None], own_start[:, None], qo_all)

    received = lax.all_to_all(partial, "tp", 0, 0, tiled=True)
    summed = jnp.zeros((tok, shard), jnp.float32)
    for g in range(nx):
        summed = summed + lax.dot_general(
            received[g], perm, (((1,), (1,)), ((), ())), preferred_element_type=jnp.float32
        )
    hidden = (tokens.astype(jnp.float32) + summed).astype(bf)
    return (hidden, kv_cache)


def solution(mesh):
    fine = Mesh(mesh.devices.reshape(*GRID, mesh.shape["tp"]), (*SEQ, "tp"))
    in_specs = (P(SEQ, "tp"), P(SEQ), P(), P(SEQ, "tp"), P(SEQ, None), P("tp", SEQ))
    out_specs = (P(SEQ, "tp"), P(SEQ, None))
    return jax.shard_map(per_device, mesh=fine, in_specs=in_specs, out_specs=out_specs, check_vma=False)
```

```python
import jax
import jax.numpy as jnp
from jax import lax
from jax.experimental import pallas as pl
from jax.experimental.pallas import tpu as pltpu
from jax.sharding import Mesh, PartitionSpec as P


HD = 256
WINDOW = 2048
SEGS = 32
GRID = (4, 2, 8, 2)
SEQ = ("x", "yh", "z", "c")


def rms_norm(values, gain):
    wide = values.astype(jnp.float32)
    scaled = wide * lax.rsqrt(jnp.mean(wide * wide, axis=-1, keepdims=True) + 1e-06)
    return (scaled * gain.astype(jnp.float32)).astype(jnp.bfloat16)


def angles(positions):
    quarter = HD // 4
    freq = 10000.0 ** (-jnp.arange(quarter, dtype=jnp.float32) / quarter)
    angle = positions[:, None] * freq
    cosine, sine = jnp.cos(angle), jnp.sin(angle)
    return jnp.concatenate([cosine, cosine], axis=1), jnp.concatenate([-sine, sine], axis=1)


def after(value, *others):
    return lax.optimization_barrier((value, *others))[0]


def spread(slab, axes, count):
    copies = jnp.broadcast_to(slab[None], (count, *slab.shape))
    return lax.all_to_all(copies, axes, 0, 0, tiled=True)


def in_order(shares, here):
    count = len(shares)
    ordered = []
    for g in range(count):
        came = (here - g) % count
        share = shares[count - 1]
        for k in range(count - 1):
            share = jnp.where(came == k, shares[k], share)
        ordered.append(share)
    return ordered


def natural_to_gathered(per, rows, ny, nz):
    nat = lax.broadcasted_iota(jnp.int32, (per, per), 0)
    gat = lax.broadcasted_iota(jnp.int32, (per, per), 1)
    half = per // 2
    core, rest = gat // half, gat % half
    place, row = rest // rows, rest % rows
    source = (((place % ny) * nz + place // ny) * 2 + core) * rows + row
    return (nat == source).astype(jnp.bfloat16)


def queries_kernel(normed_ref, cosine_ref, sine_ref, qo_ref, out_ref, weights_ref, sem):
    groups, part, cols = weights_ref.shape
    copy = pltpu.make_async_copy(qo_ref.at[:, pl.ds(0, part), :], weights_ref, sem)
    copy.start()
    copy.wait()
    raw = jnp.dot(normed_ref[0], weights_ref[0], preferred_element_type=jnp.float32)
    for g in range(1, groups):
        raw = raw + jnp.dot(normed_ref[g], weights_ref[g], preferred_element_type=jnp.float32)
    raw = raw * HD ** (-0.5)
    half = HD // 2
    for h in range(cols // HD):
        lo = raw[:, h * HD : h * HD + half]
        turned = lo * cosine_ref[...] + pltpu.roll(lo, half // 2, 1) * sine_ref[...]
        out_ref[:, h * HD : h * HD + half] = turned.astype(out_ref.dtype)
        out_ref[:, h * HD + half : (h + 1) * HD] = raw[:, h * HD + half : (h + 1) * HD].astype(
            out_ref.dtype
        )


def attend_kernel(
    queries_ref, mine_ref, partner_ref, own_ref, keys_at_ref, token_ref, first_ref, qo_ref, out_ref, weights_ref, sem
):
    groups, part, cols = weights_ref.shape
    copy = pltpu.make_async_copy(qo_ref.at[:, pl.ds(part, part), :], weights_ref, sem)
    copy.start()

    def whole(t):
        far = [ref[:, t].reshape(ref.shape[0] * ref.shape[2], ref.shape[3]) for ref in (mine_ref, partner_ref)]
        return jnp.concatenate([*far, own_ref[t]], axis=0)

    keys = jnp.concatenate([whole(0), whole(1)], axis=1)
    values = jnp.concatenate([whole(2), whole(3)], axis=1)
    at = keys_at_ref[...]
    live = (at <= token_ref[...]) & (at >= first_ref[...])
    heads = []
    for h in range(cols // HD):
        scores = lax.dot_general(
            queries_ref[:, h * HD : (h + 1) * HD],
            keys,
            (((1,), (1,)), ((), ())),
            preferred_element_type=jnp.float32,
        )
        scores = jnp.where(live, scores, -1e30)
        powered = jnp.exp(scores - jnp.max(scores, axis=1, keepdims=True))
        weights = (powered * (1.0 / jnp.sum(powered, axis=1, keepdims=True))).astype(jnp.bfloat16)
        heads.append(
            jnp.dot(weights, values, preferred_element_type=jnp.float32).astype(jnp.bfloat16)
        )
    attended = jnp.concatenate(heads, axis=1)
    copy.wait()
    for g in range(groups // 2):
        rows = jnp.concatenate([weights_ref[2 * g], weights_ref[2 * g + 1]], axis=0)
        out_ref[g] = lax.dot_general(
            attended, rows, (((1,), (1,)), ((), ())), preferred_element_type=jnp.float32
        ).astype(out_ref.dtype)


def per_device(tokens, seg_ids, norm_gain, w_query, w_keyval, w_out):
    nx, ny, nz, nc = GRID
    tok, shard = tokens.shape
    rows = w_query.shape[0]
    cols = w_query.shape[1]
    ix, iy, iz, ic = (lax.axis_index(a) for a in SEQ)
    it = lax.axis_index("tp")
    my_block = ix * ny + iy
    my_index = (my_block * nz + iz) * nc + ic
    bf = jnp.bfloat16
    both = [(0, 1), (1, 0)]

    share = 2 * HD // nx
    ids = jnp.pad(seg_ids.astype(bf)[None, :], ((0, 3), (0, 0)))
    kv_own = jnp.concatenate([lax.dynamic_slice_in_dim(w_keyval, it * share, share, 1), ids], axis=0)
    own = jnp.concatenate([w_query, w_out.T, jnp.pad(kv_own, ((0, 0), (0, cols - share)))], axis=0)
    other = lax.ppermute(own, "yh", both)
    low = jnp.where(iy == 0, own, other)
    high = jnp.where(iy == 0, other, own)

    others = [lax.ppermute(tokens, "tp", [(i, (i + k) % nx) for i in range(nx)]) for k in range(1, nx)]

    w_at, id_at = slice(2 * rows, 3 * rows), slice(3 * rows, 3 * rows + 1)
    kv_pair = jnp.concatenate([low[w_at], high[w_at], low[id_at], high[id_at]], axis=0)[:, :share]
    kv_pair = jnp.pad(kv_pair, ((0, -kv_pair.shape[0] % 8), (0, 0)))
    kv_core = spread(kv_pair, ("x", "z"), nx * nz)
    kv_twin = lax.ppermute(kv_core, "c", both)

    qo_pair = jnp.concatenate([low[:rows], high[:rows], low[rows : 2 * rows], high[rows : 2 * rows]], axis=0)
    least = (1 << 20) // (2 * nz * cols)
    qo_pair = jnp.pad(qo_pair, ((0, max(0, least - qo_pair.shape[0])), (0, 0)))
    qo_near = lax.all_gather(qo_pair, "z", axis=0, tiled=False)
    part = nz * ny * rows
    qo_send = jnp.concatenate(
        [
            qo_near[:, : ny * rows].reshape(part, cols),
            qo_near[:, ny * rows : 2 * ny * rows].reshape(part, cols),
        ],
        axis=0,
    )
    qo_all = lax.all_gather(qo_send, ("x", "c"), axis=0, tiled=False)
    kv_twin = after(kv_twin, qo_send)

    groups = in_order([tokens, *others], it)
    normed = rms_norm(jnp.concatenate(groups, axis=1), norm_gain)
    perm = natural_to_gathered(shard, rows, ny, nz)
    reordered = jnp.concatenate(
        [
            jnp.dot(normed[:, g * shard : (g + 1) * shard], perm, preferred_element_type=jnp.float32).astype(bf)
            for g in range(nx)
        ],
        axis=1,
    )
    blocks = jnp.stack([reordered[:, i * part : (i + 1) * part] for i in range(nx * nc)])
    kv_core, reordered, blocks, perm = lax.optimization_barrier((kv_core, reordered, blocks, perm))

    kv_zero = jnp.where(ic == 0, kv_core, kv_twin)
    kv_one = jnp.where(ic == 0, kv_twin, kv_core)
    all_ids = jnp.concatenate(
        [kv[:, ny * rows : ny * rows + ny] for kv in (kv_core, kv_twin)], axis=0
    ).astype(jnp.int32)
    labels = jnp.arange(SEGS, dtype=jnp.int32)
    starts = jnp.sum((all_ids.reshape(-1)[None, :] < labels[:, None]).astype(jnp.int32), axis=1)
    own_start = jnp.sum(jnp.where(seg_ids[:, None] == labels[None, :], starts[None, :], 0), axis=1)
    token_index = my_index * tok + jnp.arange(tok, dtype=jnp.int32)
    cosine, sine = angles((token_index - own_start).astype(jnp.float32))

    kv_rows = jnp.stack(
        [
            kv[:, : ny * rows].reshape(nx, part, share)
            for kv in (kv_zero, kv_one)
        ],
        axis=1,
    ).reshape(nx * nc * part, share)
    kv_raw = jnp.dot(reordered, kv_rows, preferred_element_type=jnp.float32)
    quarter = HD // 4
    swapped = jnp.concatenate([kv_raw[:, quarter:], kv_raw[:, :quarter]], axis=1)
    kv_share = jnp.where(it == 0, kv_raw * cosine + swapped * sine, kv_raw).astype(bf)

    block = nz * nc
    devices = nx * ny * block
    before = lax.ppermute(kv_share, SEQ, [(i, i + block) for i in range(devices - block)])
    chips = jnp.arange(nz, dtype=jnp.int32)
    to_send = jnp.where((chips > iz)[:, None, None], kv_share[None], before[None])
    to_send = jnp.broadcast_to(to_send[:, None], (nz, nx, tok, share)).reshape(nz * nx, tok, share)
    mine = lax.all_to_all(to_send, ("z", "tp"), 0, 0, tiled=True).reshape(nz, nx, tok, share)
    rest = [lax.ppermute(kv_share, "tp", [(i, (i + k) % nx) for i in range(nx)]) for k in range(1, nx)]
    own_kv = jnp.stack(in_order([kv_share, *rest], it))
    kv_cache = jnp.concatenate(list(own_kv), axis=1)
    at_self = (chips == iz)[:, None, None, None] & (ic == 0)
    partner = lax.ppermute(jnp.where(at_self, own_kv[None], mine), "c", both)
    block_of_mine = my_block - (chips >= iz).astype(jnp.int32)
    block_of_partner = my_block - jnp.where(ic == 1, chips > iz, chips >= iz).astype(jnp.int32)
    first_of_mine = ((block_of_mine * nz + chips) * nc + ic) * tok
    first_of_partner = ((block_of_partner * nz + chips) * nc + 1 - ic) * tok
    firsts = jnp.concatenate([first_of_mine, first_of_partner, my_index[None] * tok])
    keys_at = (firsts[:, None] + jnp.arange(tok, dtype=jnp.int32)[None, :]).reshape(1, -1)

    vmem = pl.BlockSpec(memory_space=pltpu.VMEM)
    hbm = pl.BlockSpec(memory_space=pl.ANY)
    scratch = [pltpu.VMEM((nx * nc, part, cols), bf), pltpu.SemaphoreType.DMA]
    queries = pl.pallas_call(
        queries_kernel,
        out_shape=jax.ShapeDtypeStruct((tok, cols), bf),
        in_specs=[vmem, vmem, vmem, hbm],
        out_specs=vmem,
        scratch_shapes=scratch,
        name="queries",
    )(blocks, cosine, sine, qo_all)
    reach_back = jnp.maximum(own_start, token_index - (WINDOW - 1))
    partial = pl.pallas_call(
        attend_kernel,
        out_shape=jax.ShapeDtypeStruct((nx, tok, shard), bf),
        in_specs=[vmem] * 7 + [hbm],
        out_specs=vmem,
        scratch_shapes=scratch,
        name="attend",
    )(queries, mine, partner, own_kv, keys_at, token_index[:, None], reach_back[:, None], qo_all)

    received = lax.all_to_all(partial, "tp", 0, 0, tiled=True)
    summed = jnp.zeros((tok, shard), jnp.float32)
    for g in range(nx):
        summed = summed + lax.dot_general(
            received[g], perm, (((1,), (1,)), ((), ())), preferred_element_type=jnp.float32
        )
    hidden = (tokens.astype(jnp.float32) + summed).astype(bf)
    return (hidden, kv_cache)


def solution(mesh):
    fine = Mesh(mesh.devices.reshape(*GRID, mesh.shape["tp"]), (*SEQ, "tp"))
    in_specs = (P(SEQ, "tp"), P(SEQ), P(), P(SEQ, "tp"), P(SEQ, None), P("tp", SEQ))
    out_specs = (P(SEQ, "tp"), P(SEQ, None))
    return jax.shard_map(per_device, mesh=fine, in_specs=in_specs, out_specs=out_specs, check_vma=False)
```

```python
import jax
import jax.numpy as jnp
from jax import lax
from jax.experimental import pallas as pl
from jax.experimental.pallas import tpu as pltpu
from jax.sharding import Mesh, PartitionSpec as P


HD = 256
WINDOW = 2048
SEGS = 32
GRID = (4, 2, 8, 2)
SEQ = ("x", "yh", "z", "c")


def rms_norm(values, gain):
    wide = values.astype(jnp.float32)
    scaled = wide * lax.rsqrt(jnp.mean(wide * wide, axis=-1, keepdims=True) + 1e-06)
    return (scaled * gain.astype(jnp.float32)).astype(jnp.bfloat16)


def angles(positions):
    quarter = HD // 4
    freq = 10000.0 ** (-jnp.arange(quarter, dtype=jnp.float32) / quarter)
    angle = positions[:, None] * freq
    cosine, sine = jnp.cos(angle), jnp.sin(angle)
    return jnp.concatenate([cosine, cosine], axis=1), jnp.concatenate([-sine, sine], axis=1)


def after(value, *others):
    return lax.optimization_barrier((value, *others))[0]


def spread(slab, axes, count):
    copies = jnp.broadcast_to(slab[None], (count, *slab.shape))
    return lax.all_to_all(copies, axes, 0, 0, tiled=True)


def in_order(shares, here):
    count = len(shares)
    ordered = []
    for g in range(count):
        came = (here - g) % count
        share = shares[count - 1]
        for k in range(count - 1):
            share = jnp.where(came == k, shares[k], share)
        ordered.append(share)
    return ordered


def natural_to_gathered(per, rows, ny, nz):
    nat = lax.broadcasted_iota(jnp.int32, (per, per), 0)
    gat = lax.broadcasted_iota(jnp.int32, (per, per), 1)
    half = per // 2
    core, rest = gat // half, gat % half
    place, row = rest // rows, rest % rows
    source = (((place % ny) * nz + place // ny) * 2 + core) * rows + row
    return (nat == source).astype(jnp.bfloat16)


def queries_kernel(normed_ref, cosine_ref, sine_ref, qo_ref, out_ref, weights_ref, sem):
    groups, part, cols = weights_ref.shape
    copy = pltpu.make_async_copy(qo_ref.at[:, pl.ds(0, part), :], weights_ref, sem)
    copy.start()
    copy.wait()
    raw = jnp.dot(normed_ref[0], weights_ref[0], preferred_element_type=jnp.float32)
    for g in range(1, groups):
        raw = raw + jnp.dot(normed_ref[g], weights_ref[g], preferred_element_type=jnp.float32)
    raw = raw * HD ** (-0.5)
    half = HD // 2
    for h in range(cols // HD):
        lo = raw[:, h * HD : h * HD + half]
        turned = lo * cosine_ref[...] + pltpu.roll(lo, half // 2, 1) * sine_ref[...]
        out_ref[:, h * HD : h * HD + half] = turned.astype(out_ref.dtype)
        out_ref[:, h * HD + half : (h + 1) * HD] = raw[:, h * HD + half : (h + 1) * HD].astype(
            out_ref.dtype
        )


def attend_kernel(
    queries_ref, mine_ref, partner_ref, own_ref, keys_at_ref, token_ref, first_ref, qo_ref, out_ref, weights_ref, sem
):
    groups, part, cols = weights_ref.shape
    copy = pltpu.make_async_copy(qo_ref.at[:, pl.ds(part, part), :], weights_ref, sem)
    copy.start()

    def whole(t):
        far = [ref[:, t].reshape(ref.shape[0] * ref.shape[2], ref.shape[3]) for ref in (mine_ref, partner_ref)]
        return jnp.concatenate([*far, own_ref[t]], axis=0)

    keys = jnp.concatenate([whole(0), whole(1)], axis=1)
    values = jnp.concatenate([whole(2), whole(3)], axis=1)
    at = keys_at_ref[...]
    live = (at <= token_ref[...]) & (at >= first_ref[...])
    heads = []
    for h in range(cols // HD):
        scores = lax.dot_general(
            queries_ref[:, h * HD : (h + 1) * HD],
            keys,
            (((1,), (1,)), ((), ())),
            preferred_element_type=jnp.float32,
        )
        scores = jnp.where(live, scores, -1e30)
        powered = jnp.exp(scores - jnp.max(scores, axis=1, keepdims=True))
        weights = (powered * (1.0 / jnp.sum(powered, axis=1, keepdims=True))).astype(jnp.bfloat16)
        heads.append(
            jnp.dot(weights, values, preferred_element_type=jnp.float32).astype(jnp.bfloat16)
        )
    attended = jnp.concatenate(heads, axis=1)
    copy.wait()
    for g in range(groups // 2):
        rows = jnp.concatenate([weights_ref[2 * g], weights_ref[2 * g + 1]], axis=0)
        out_ref[g] = lax.dot_general(
            attended, rows, (((1,), (1,)), ((), ())), preferred_element_type=jnp.float32
        ).astype(out_ref.dtype)


def per_device(tokens, seg_ids, norm_gain, w_query, w_keyval, w_out):
    nx, ny, nz, nc = GRID
    tok, shard = tokens.shape
    rows = w_query.shape[0]
    cols = w_query.shape[1]
    ix, iy, iz, ic = (lax.axis_index(a) for a in SEQ)
    it = lax.axis_index("tp")
    my_block = ix * ny + iy
    my_index = (my_block * nz + iz) * nc + ic
    bf = jnp.bfloat16
    both = [(0, 1), (1, 0)]

    share = 2 * HD // nx
    ids = jnp.pad(seg_ids.astype(bf)[None, :], ((0, 3), (0, 0)))
    kv_slab = jnp.concatenate([lax.dynamic_slice_in_dim(w_keyval, it * share, share, 1), ids], axis=0)
    kv_core = spread(kv_slab, ("x", "yh", "z"), nx * ny * nz)
    kv_twin = lax.ppermute(kv_core, "c", both)

    others = [lax.ppermute(tokens, "tp", [(i, (i + k) % nx) for i in range(nx)]) for k in range(1, nx)]

    qo_own = jnp.concatenate([w_query, w_out.T], axis=0)
    qo_other = lax.ppermute(qo_own, "yh", both)
    low = jnp.where(iy == 0, qo_own, qo_other)
    high = jnp.where(iy == 0, qo_other, qo_own)
    qo_pair = jnp.concatenate([low[:rows], high[:rows], low[rows:], high[rows:]], axis=0)
    least = (1 << 20) // (2 * nz * cols)
    qo_pair = jnp.pad(qo_pair, ((0, max(0, least - qo_pair.shape[0])), (0, 0)))
    qo_near = lax.all_gather(qo_pair, "z", axis=0, tiled=False)
    groups = in_order([tokens, *others], it)
    normed = rms_norm(jnp.concatenate(groups, axis=1), norm_gain)

    kv_zero = jnp.where(ic == 0, kv_core, kv_twin)
    kv_one = jnp.where(ic == 0, kv_twin, kv_core)
    all_ids = jnp.concatenate([kv_core[:, rows], kv_twin[:, rows]], axis=0).astype(jnp.int32)
    labels = jnp.arange(SEGS, dtype=jnp.int32)
    starts = jnp.sum((all_ids.reshape(-1)[None, :] < labels[:, None]).astype(jnp.int32), axis=1)
    own_start = jnp.sum(jnp.where(seg_ids[:, None] == labels[None, :], starts[None, :], 0), axis=1)
    token_index = my_index * tok + jnp.arange(tok, dtype=jnp.int32)
    cosine, sine = angles((token_index - own_start).astype(jnp.float32))

    kv_rows = jnp.stack([kv_zero[:, :rows], kv_one[:, :rows]], axis=1).reshape(nx * shard, share)
    kv_raw = jnp.dot(normed, kv_rows, preferred_element_type=jnp.float32)
    quarter = HD // 4
    swapped = jnp.concatenate([kv_raw[:, quarter:], kv_raw[:, :quarter]], axis=1)
    kv_share = jnp.where(it == 0, kv_raw * cosine + swapped * sine, kv_raw).astype(bf)

    block = nz * nc
    devices = nx * ny * block
    before = lax.ppermute(kv_share, SEQ, [(i, i + block) for i in range(devices - block)])
    chips = jnp.arange(nz, dtype=jnp.int32)
    to_send = jnp.where((chips > iz)[:, None, None], kv_share[None], before[None])
    to_send = jnp.broadcast_to(to_send[:, None], (nz, nx, tok, share)).reshape(nz * nx, tok, share)
    mine = lax.all_to_all(to_send, ("z", "tp"), 0, 0, tiled=True).reshape(nz, nx, tok, share)
    rest = [lax.ppermute(kv_share, "tp", [(i, (i + k) % nx) for i in range(nx)]) for k in range(1, nx)]
    own_kv = jnp.stack(in_order([kv_share, *rest], it))
    kv_cache = jnp.concatenate(list(own_kv), axis=1)
    at_self = (chips == iz)[:, None, None, None] & (ic == 0)
    partner = lax.ppermute(jnp.where(at_self, own_kv[None], mine), "c", both)
    part = nz * ny * rows
    qo_near = after(qo_near, to_send)
    qo_send = jnp.concatenate(
        [
            qo_near[:, : ny * rows].reshape(part, cols),
            qo_near[:, ny * rows : 2 * ny * rows].reshape(part, cols),
        ],
        axis=0,
    )
    qo_all = lax.all_gather(qo_send, ("x", "c"), axis=0, tiled=False)
    perm = natural_to_gathered(shard, rows, ny, nz)
    normed = after(normed, to_send)
    blocks = []
    for g in range(nx):
        turned = jnp.dot(normed[:, g * shard : (g + 1) * shard], perm, preferred_element_type=jnp.float32)
        blocks += [turned[:, :part].astype(bf), turned[:, part:].astype(bf)]
    blocks = jnp.stack(blocks)
    block_of_mine = my_block - (chips >= iz).astype(jnp.int32)
    block_of_partner = my_block - jnp.where(ic == 1, chips > iz, chips >= iz).astype(jnp.int32)
    first_of_mine = ((block_of_mine * nz + chips) * nc + ic) * tok
    first_of_partner = ((block_of_partner * nz + chips) * nc + 1 - ic) * tok
    firsts = jnp.concatenate([first_of_mine, first_of_partner, my_index[None] * tok])
    keys_at = (firsts[:, None] + jnp.arange(tok, dtype=jnp.int32)[None, :]).reshape(1, -1)

    vmem = pl.BlockSpec(memory_space=pltpu.VMEM)
    hbm = pl.BlockSpec(memory_space=pl.ANY)
    scratch = [pltpu.VMEM((nx * nc, part, cols), bf), pltpu.SemaphoreType.DMA]
    queries = pl.pallas_call(
        queries_kernel,
        out_shape=jax.ShapeDtypeStruct((tok, cols), bf),
        in_specs=[vmem, vmem, vmem, hbm],
        out_specs=vmem,
        scratch_shapes=scratch,
        name="queries",
    )(blocks, cosine, sine, qo_all)
    reach_back = jnp.maximum(own_start, token_index - (WINDOW - 1))
    partial = pl.pallas_call(
        attend_kernel,
        out_shape=jax.ShapeDtypeStruct((nx, tok, shard), bf),
        in_specs=[vmem] * 7 + [hbm],
        out_specs=vmem,
        scratch_shapes=scratch,
        name="attend",
    )(queries, mine, partner, own_kv, keys_at, token_index[:, None], reach_back[:, None], qo_all)

    received = lax.all_to_all(partial, "tp", 0, 0, tiled=True)
    summed = jnp.zeros((tok, shard), jnp.float32)
    for g in range(nx):
        summed = summed + lax.dot_general(
            received[g], perm, (((1,), (1,)), ((), ())), preferred_element_type=jnp.float32
        )
    hidden = (tokens.astype(jnp.float32) + summed).astype(bf)
    return (hidden, kv_cache)


def solution(mesh):
    fine = Mesh(mesh.devices.reshape(*GRID, mesh.shape["tp"]), (*SEQ, "tp"))
    in_specs = (P(SEQ, "tp"), P(SEQ), P(), P(SEQ, "tp"), P(SEQ, None), P("tp", SEQ))
    out_specs = (P(SEQ, "tp"), P(SEQ, None))
    return jax.shard_map(per_device, mesh=fine, in_specs=in_specs, out_specs=out_specs, check_vma=False)
```

```python
import jax
import jax.numpy as jnp
from jax import lax
from jax.experimental import pallas as pl
from jax.experimental.pallas import tpu as pltpu
from jax.sharding import Mesh, PartitionSpec as P


HD = 256
WINDOW = 2048
SEGS = 32
GRID = (4, 2, 8, 2)
SEQ = ("x", "yh", "z", "c")


def rms_norm(values, gain):
    wide = values.astype(jnp.float32)
    scaled = wide * lax.rsqrt(jnp.mean(wide * wide, axis=-1, keepdims=True) + 1e-06)
    return (scaled * gain.astype(jnp.float32)).astype(jnp.bfloat16)


def angles(positions):
    quarter = HD // 4
    freq = 10000.0 ** (-jnp.arange(quarter, dtype=jnp.float32) / quarter)
    angle = positions[:, None] * freq
    cosine, sine = jnp.cos(angle), jnp.sin(angle)
    return jnp.concatenate([cosine, cosine], axis=1), jnp.concatenate([-sine, sine], axis=1)


def after(value, *others):
    return lax.optimization_barrier((value, *others))[0]


def spread(slab, axes, count):
    copies = jnp.broadcast_to(slab[None], (count, *slab.shape))
    return lax.all_to_all(copies, axes, 0, 0, tiled=True)


def in_order(shares, here):
    count = len(shares)
    ordered = []
    for g in range(count):
        came = (here - g) % count
        share = shares[count - 1]
        for k in range(count - 1):
            share = jnp.where(came == k, shares[k], share)
        ordered.append(share)
    return ordered


def natural_to_gathered(per, rows):
    nat = lax.broadcasted_iota(jnp.int32, (per, per), 0)
    gat = lax.broadcasted_iota(jnp.int32, (per, per), 1)
    half = per // 2
    core, rest = gat // half, gat % half
    place, row = rest // rows, rest % rows
    source = (place * 2 + core) * rows + row
    return (nat == source).astype(jnp.bfloat16)


def fetch(qo_ref, at, weights_ref, sems):
    groups = qo_ref.shape[0]
    part = qo_ref.shape[1] // 2
    copies = [
        pltpu.make_async_copy(
            qo_ref.at[g, pl.ds(at * part, part), :], weights_ref.at[pl.ds(g * part, part), :], sems.at[g]
        )
        for g in range(groups)
    ]
    for copy in copies:
        copy.start()
    return copies


def queries_kernel(normed_ref, cosine_ref, sine_ref, qo_ref, out_ref, weights_ref, sems):
    for copy in fetch(qo_ref, 0, weights_ref, sems):
        copy.wait()
    raw = jnp.dot(normed_ref[...], weights_ref[...], preferred_element_type=jnp.float32) * HD ** (-0.5)
    half = HD // 2
    for h in range(raw.shape[1] // HD):
        lo = raw[:, h * HD : h * HD + half]
        turned = lo * cosine_ref[...] + pltpu.roll(lo, half // 2, 1) * sine_ref[...]
        out_ref[:, h * HD : h * HD + half] = turned.astype(out_ref.dtype)
        out_ref[:, h * HD + half : (h + 1) * HD] = raw[:, h * HD + half : (h + 1) * HD].astype(
            out_ref.dtype
        )


def attend_kernel(
    queries_ref, mine_ref, partner_ref, own_ref, keys_at_ref, token_ref, first_ref, out_ref
):
    def whole(t):
        far = [ref[:, t].reshape(ref.shape[0] * ref.shape[2], ref.shape[3]) for ref in (mine_ref, partner_ref)]
        return jnp.concatenate([*far, own_ref[t]], axis=0)

    keys = jnp.concatenate([whole(0), whole(1)], axis=1)
    values = jnp.concatenate([whole(2), whole(3)], axis=1)
    at = keys_at_ref[...]
    live = (at <= token_ref[...]) & (at >= first_ref[...])
    for h in range(out_ref.shape[1] // HD):
        scores = lax.dot_general(
            queries_ref[:, h * HD : (h + 1) * HD],
            keys,
            (((1,), (1,)), ((), ())),
            preferred_element_type=jnp.float32,
        )
        scores = jnp.where(live, scores, -1e30)
        powered = jnp.exp(scores - jnp.max(scores, axis=1, keepdims=True))
        weights = (powered * (1.0 / jnp.sum(powered, axis=1, keepdims=True))).astype(jnp.bfloat16)
        out_ref[:, h * HD : (h + 1) * HD] = jnp.dot(
            weights, values, preferred_element_type=jnp.float32
        ).astype(out_ref.dtype)


def finish_kernel(every_ref, perm_ref, tokens_ref, qo_ref, out_ref, weights_ref, sems):
    copies = fetch(qo_ref, 1, weights_ref, sems)
    shard = out_ref.shape[1]
    cols = qo_ref.shape[2]
    turn = lambda a, b: lax.dot_general(a, b, (((1,), (1,)), ((), ())), preferred_element_type=jnp.float32)
    for copy in copies:
        copy.wait()
    summed = jnp.zeros(out_ref.shape, jnp.float32)
    for b in range(weights_ref.shape[0] // shard):
        summed = summed + turn(every_ref[:, b * cols : (b + 1) * cols], weights_ref[b * shard : (b + 1) * shard, :])
    first = summed.astype(jnp.bfloat16)
    rest = summed - first.astype(jnp.float32)
    second = rest.astype(jnp.bfloat16)
    third = (rest - second.astype(jnp.float32)).astype(jnp.bfloat16)
    perm = perm_ref[...]
    natural = turn(first, perm) + (turn(second, perm) + turn(third, perm))
    out_ref[...] = (tokens_ref[...].astype(jnp.float32) + natural).astype(out_ref.dtype)


def per_device(tokens, seg_ids, norm_gain, w_query, w_keyval, w_out):
    nx, ny, nz, nc = GRID
    tok, shard = tokens.shape
    rows = w_query.shape[0]
    cols = w_query.shape[1]
    ix, iy, iz, ic = (lax.axis_index(a) for a in SEQ)
    it = lax.axis_index("tp")
    my_block = ix * ny + iy
    my_index = (my_block * nz + iz) * nc + ic
    bf = jnp.bfloat16
    both = [(0, 1), (1, 0)]

    share = 2 * HD // nx
    ids = jnp.pad(seg_ids.astype(bf)[None, :], ((0, 3), (0, 0)))
    kv_slab = jnp.concatenate([lax.dynamic_slice_in_dim(w_keyval, it * share, share, 1), ids], axis=0)
    kv_core = spread(kv_slab, ("x", "yh", "z"), nx * ny * nz)
    kv_twin = lax.ppermute(kv_core, "c", both)

    others = [lax.ppermute(tokens, "tp", [(i, (i + k) % nx) for i in range(nx)]) for k in range(1, nx)]

    diagonal = [(a * nx + b, b * nx + a) for a in range(nx) for b in range(nx)]
    o_rows = lax.ppermute(w_out.T, ("x", "tp"), diagonal)
    qo_slab = jnp.concatenate([w_query, o_rows], axis=0)
    qo_near = spread(after(qo_slab, kv_core), ("yh", "z"), ny * nz)

    groups = in_order([tokens, *others], it)
    normed = rms_norm(jnp.concatenate(groups, axis=1), norm_gain)

    kv_zero = jnp.where(ic == 0, kv_core, kv_twin)
    kv_one = jnp.where(ic == 0, kv_twin, kv_core)
    all_ids = jnp.concatenate([kv_core[:, rows], kv_twin[:, rows]], axis=0).astype(jnp.int32)
    labels = jnp.arange(SEGS, dtype=jnp.int32)
    starts = jnp.sum((all_ids.reshape(-1)[None, :] < labels[:, None]).astype(jnp.int32), axis=1)
    own_start = jnp.sum(jnp.where(seg_ids[:, None] == labels[None, :], starts[None, :], 0), axis=1)
    token_index = my_index * tok + jnp.arange(tok, dtype=jnp.int32)
    cosine, sine = angles((token_index - own_start).astype(jnp.float32))

    kv_rows = jnp.stack([kv_zero[:, :rows], kv_one[:, :rows]], axis=1).reshape(nx * shard, share)
    kv_raw = jnp.dot(normed, kv_rows, preferred_element_type=jnp.float32)
    quarter = HD // 4
    swapped = jnp.concatenate([kv_raw[:, quarter:], kv_raw[:, :quarter]], axis=1)
    kv_share = jnp.where(it == 0, kv_raw * cosine + swapped * sine, kv_raw).astype(bf)

    block = nz * nc
    devices = nx * ny * block
    before = lax.ppermute(kv_share, SEQ, [(i, i + block) for i in range(devices - block)])
    chips = jnp.arange(nz, dtype=jnp.int32)
    to_send = jnp.where((chips > iz)[:, None, None], kv_share[None], before[None])
    to_send = jnp.broadcast_to(to_send[:, None], (nz, nx, tok, share)).reshape(nz * nx, tok, share)
    mine = lax.all_to_all(to_send, ("z", "tp"), 0, 0, tiled=True).reshape(nz, nx, tok, share)
    rest = [lax.ppermute(kv_share, "tp", [(i, (i + k) % nx) for i in range(nx)]) for k in range(1, nx)]
    own_kv = jnp.stack(in_order([kv_share, *rest], it))
    kv_cache = jnp.concatenate(list(own_kv), axis=1)
    at_self = (chips == iz)[:, None, None, None] & (ic == 0)
    partner = lax.ppermute(jnp.where(at_self, own_kv[None], mine), "c", both)
    part = nz * ny * rows
    qo_send = jnp.concatenate([qo_near[:, :rows].reshape(part, cols), qo_near[:, rows:].reshape(part, cols)], axis=0)
    qo_all = lax.all_gather(qo_send, ("x", "c"), axis=0, tiled=False)
    perm = natural_to_gathered(shard, rows)
    normed = after(normed, to_send)
    reordered = jnp.concatenate(
        [
            jnp.dot(normed[:, g * shard : (g + 1) * shard], perm, preferred_element_type=jnp.float32).astype(bf)
            for g in range(nx)
        ],
        axis=1,
    )
    block_of_mine = my_block - (chips >= iz).astype(jnp.int32)
    block_of_partner = my_block - jnp.where(ic == 1, chips > iz, chips >= iz).astype(jnp.int32)
    first_of_mine = ((block_of_mine * nz + chips) * nc + ic) * tok
    first_of_partner = ((block_of_partner * nz + chips) * nc + 1 - ic) * tok
    firsts = jnp.concatenate([first_of_mine, first_of_partner, my_index[None] * tok])
    keys_at = (firsts[:, None] + jnp.arange(tok, dtype=jnp.int32)[None, :]).reshape(1, -1)

    vmem = pl.BlockSpec(memory_space=pltpu.VMEM)
    hbm = pl.BlockSpec(memory_space=pl.ANY)
    scratch = [pltpu.VMEM((nx * nc * part, cols), bf), pltpu.SemaphoreType.DMA((nx * nc,))]
    queries = pl.pallas_call(
        queries_kernel,
        out_shape=jax.ShapeDtypeStruct((tok, cols), bf),
        in_specs=[vmem, vmem, vmem, hbm],
        out_specs=vmem,
        scratch_shapes=scratch,
        name="queries",
    )(reordered, cosine, sine, qo_all)
    reach_back = jnp.maximum(own_start, token_index - (WINDOW - 1))
    attended = pl.pallas_call(
        attend_kernel,
        out_shape=jax.ShapeDtypeStruct((tok, cols), bf),
        in_specs=[vmem] * 7,
        out_specs=vmem,
        name="attend",
    )(queries, mine, partner, own_kv, keys_at, token_index[:, None], reach_back[:, None])

    every = lax.all_gather(attended, "tp", axis=1, tiled=True)
    hidden = pl.pallas_call(
        finish_kernel,
        out_shape=jax.ShapeDtypeStruct((tok, shard), bf),
        in_specs=[vmem, vmem, vmem, hbm],
        out_specs=vmem,
        scratch_shapes=scratch,
        name="finish",
    )(every, perm, tokens, qo_all)
    return (hidden, kv_cache)


def solution(mesh):
    fine = Mesh(mesh.devices.reshape(*GRID, mesh.shape["tp"]), (*SEQ, "tp"))
    in_specs = (P(SEQ, "tp"), P(SEQ), P(), P(SEQ, "tp"), P(SEQ, None), P("tp", SEQ))
    out_specs = (P(SEQ, "tp"), P(SEQ, None))
    return jax.shard_map(per_device, mesh=fine, in_specs=in_specs, out_specs=out_specs, check_vma=False)
```

```python
import jax
import jax.numpy as jnp
from jax import lax
from jax.experimental import pallas as pl
from jax.experimental.pallas import tpu as pltpu
from jax.sharding import Mesh, PartitionSpec as P


HD = 256
WINDOW = 2048
SEGS = 32
GRID = (4, 2, 8, 2)
SEQ = ("x", "yh", "z", "c")


def rms_norm(values, gain):
    wide = values.astype(jnp.float32)
    scaled = wide * lax.rsqrt(jnp.mean(wide * wide, axis=-1, keepdims=True) + 1e-06)
    return (scaled * gain.astype(jnp.float32)).astype(jnp.bfloat16)


def angles(positions):
    quarter = HD // 4
    freq = 10000.0 ** (-jnp.arange(quarter, dtype=jnp.float32) / quarter)
    angle = positions[:, None] * freq
    cosine, sine = jnp.cos(angle), jnp.sin(angle)
    return jnp.concatenate([cosine, cosine], axis=1), jnp.concatenate([-sine, sine], axis=1)


def after(value, *others):
    return lax.optimization_barrier((value, *others))[0]


def spread(slab, axes, count):
    copies = jnp.broadcast_to(slab[None], (count, *slab.shape))
    return lax.all_to_all(copies, axes, 0, 0, tiled=True)


def in_order(shares, here):
    count = len(shares)
    ordered = []
    for g in range(count):
        came = (here - g) % count
        share = shares[count - 1]
        for k in range(count - 1):
            share = jnp.where(came == k, shares[k], share)
        ordered.append(share)
    return ordered


def natural_to_gathered(per, rows, slab):
    width = per // rows * slab
    nat = lax.broadcasted_iota(jnp.int32, (per, width), 0)
    gat = lax.broadcasted_iota(jnp.int32, (per, width), 1)
    half = width // 2
    core, rest = gat // half, gat % half
    place, row = rest // slab, rest % slab
    source = (place * 2 + core) * rows + row
    return ((nat == source) & (row < rows)).astype(jnp.bfloat16)


def turned(values, hot):
    per = hot.shape[0]
    return jnp.concatenate(
        [
            jnp.dot(values[:, g : g + per], hot, preferred_element_type=jnp.float32).astype(jnp.bfloat16)
            for g in range(0, values.shape[1], per)
        ],
        axis=1,
    )


def fetch(qo_ref, at, weights_ref, sems):
    groups = qo_ref.shape[0]
    part = qo_ref.shape[1] // 2
    copies = [
        pltpu.make_async_copy(
            qo_ref.at[g, pl.ds(at * part, part), :], weights_ref.at[pl.ds(g * part, part), :], sems.at[g]
        )
        for g in range(groups)
    ]
    for copy in copies:
        copy.start()
    return copies


def queries_kernel(normed_ref, cosine_ref, sine_ref, qo_ref, out_ref, weights_ref, sems):
    for copy in fetch(qo_ref, 0, weights_ref, sems):
        copy.wait()
    raw = jnp.dot(normed_ref[...], weights_ref[...], preferred_element_type=jnp.float32) * HD ** (-0.5)
    half = HD // 2
    for h in range(raw.shape[1] // HD):
        lo = raw[:, h * HD : h * HD + half]
        turned = lo * cosine_ref[...] + pltpu.roll(lo, half // 2, 1) * sine_ref[...]
        out_ref[:, h * HD : h * HD + half] = turned.astype(out_ref.dtype)
        out_ref[:, h * HD + half : (h + 1) * HD] = raw[:, h * HD + half : (h + 1) * HD].astype(
            out_ref.dtype
        )


def attend_kernel(
    queries_ref, mine_ref, partner_ref, own_ref, keys_at_ref, token_ref, first_ref, qo_ref, out_ref, weights_ref, sems
):
    copies = fetch(qo_ref, 1, weights_ref, sems)

    def whole(t):
        far = [ref[:, t].reshape(ref.shape[0] * ref.shape[2], ref.shape[3]) for ref in (mine_ref, partner_ref)]
        return jnp.concatenate([*far, own_ref[t]], axis=0)

    keys = jnp.concatenate([whole(0), whole(1)], axis=1)
    values = jnp.concatenate([whole(2), whole(3)], axis=1)
    at = keys_at_ref[...]
    live = (at <= token_ref[...]) & (at >= first_ref[...])
    heads = []
    for h in range(queries_ref.shape[1] // HD):
        scores = lax.dot_general(
            queries_ref[:, h * HD : (h + 1) * HD],
            keys,
            (((1,), (1,)), ((), ())),
            preferred_element_type=jnp.float32,
        )
        scores = jnp.where(live, scores, -1e30)
        powered = jnp.exp(scores - jnp.max(scores, axis=1, keepdims=True))
        weights = (powered * (1.0 / jnp.sum(powered, axis=1, keepdims=True))).astype(jnp.bfloat16)
        heads.append(
            jnp.dot(weights, values, preferred_element_type=jnp.float32).astype(jnp.bfloat16)
        )
    attended = jnp.concatenate(heads, axis=1)
    shard = out_ref.shape[2]
    for copy in copies:
        copy.wait()
    for g in range(out_ref.shape[0]):
        out_ref[g] = lax.dot_general(
            attended,
            weights_ref[g * shard : (g + 1) * shard, :],
            (((1,), (1,)), ((), ())),
            preferred_element_type=jnp.float32,
        ).astype(out_ref.dtype)


def per_device(tokens, seg_ids, norm_gain, w_query, w_keyval, w_out):
    nx, ny, nz, nc = GRID
    tok, shard = tokens.shape
    rows = w_query.shape[0]
    cols = w_query.shape[1]
    ix, iy, iz, ic = (lax.axis_index(a) for a in SEQ)
    it = lax.axis_index("tp")
    my_block = ix * ny + iy
    my_index = (my_block * nz + iz) * nc + ic
    bf = jnp.bfloat16
    both = [(0, 1), (1, 0)]

    share = 2 * HD // nx
    slab = rows + 4
    ids = jnp.pad(seg_ids.astype(bf)[None, :], ((0, 31 - rows), (0, 0)))
    kv_slab = jnp.concatenate([lax.dynamic_slice_in_dim(w_keyval, it * share, share, 1), ids], axis=0)
    folded = jnp.concatenate([kv_slab[i : i + 8] for i in range(0, 32, 8)], axis=1)
    near = spread(jnp.concatenate([w_query, w_out.T, folded], axis=0), ("yh", "z"), ny * nz)

    others = [lax.ppermute(tokens, "tp", [(i, (i + k) % nx) for i in range(nx)]) for k in range(1, nx)]

    kv_near = jnp.concatenate(
        [near[:, 2 * rows :, i * share : (i + 1) * share] for i in range(slab // 8)], axis=1
    )
    kv_all = spread(kv_near, ("x", "c"), nx * nc)
    part = nz * ny * rows
    qo_send = jnp.concatenate(
        [near[:, :rows].reshape(part, cols), near[:, rows : 2 * rows].reshape(part, cols)], axis=0
    )
    qo_all = lax.all_gather(qo_send, ("x", "c"), axis=0, tiled=False)

    groups = in_order([tokens, *others], it)
    normed = rms_norm(jnp.concatenate(groups, axis=1), norm_gain)
    padded = turned(normed, natural_to_gathered(shard, rows, slab))
    kv_all, padded = lax.optimization_barrier((kv_all, padded))

    all_ids = kv_all[:, :, rows].astype(jnp.int32)
    labels = jnp.arange(SEGS, dtype=jnp.int32)
    starts = jnp.sum((all_ids.reshape(-1)[None, :] < labels[:, None]).astype(jnp.int32), axis=1)
    own_start = jnp.sum(jnp.where(seg_ids[:, None] == labels[None, :], starts[None, :], 0), axis=1)
    token_index = my_index * tok + jnp.arange(tok, dtype=jnp.int32)
    cosine, sine = angles((token_index - own_start).astype(jnp.float32))

    kv_raw = jnp.dot(
        padded, kv_all.reshape(nx * nc * ny * nz * slab, share), preferred_element_type=jnp.float32
    )
    quarter = HD // 4
    swapped = jnp.concatenate([kv_raw[:, quarter:], kv_raw[:, :quarter]], axis=1)
    kv_share = jnp.where(it == 0, kv_raw * cosine + swapped * sine, kv_raw).astype(bf)

    block = nz * nc
    devices = nx * ny * block
    before = lax.ppermute(kv_share, SEQ, [(i, i + block) for i in range(devices - block)])
    chips = jnp.arange(nz, dtype=jnp.int32)
    to_send = jnp.where((chips > iz)[:, None, None], kv_share[None], before[None])
    to_send = jnp.broadcast_to(to_send[:, None], (nz, nx, tok, share)).reshape(nz * nx, tok, share)
    mine = lax.all_to_all(to_send, ("z", "tp"), 0, 0, tiled=True).reshape(nz, nx, tok, share)
    rest = [lax.ppermute(kv_share, "tp", [(i, (i + k) % nx) for i in range(nx)]) for k in range(1, nx)]
    own_kv = jnp.stack(in_order([kv_share, *rest], it))
    kv_cache = jnp.concatenate(list(own_kv), axis=1)
    at_self = (chips == iz)[:, None, None, None] & (ic == 0)
    partner = lax.ppermute(jnp.where(at_self, own_kv[None], mine), "c", both)
    perm = natural_to_gathered(shard, rows, rows)
    reordered = turned(after(normed, to_send), perm)
    block_of_mine = my_block - (chips >= iz).astype(jnp.int32)
    block_of_partner = my_block - jnp.where(ic == 1, chips > iz, chips >= iz).astype(jnp.int32)
    first_of_mine = ((block_of_mine * nz + chips) * nc + ic) * tok
    first_of_partner = ((block_of_partner * nz + chips) * nc + 1 - ic) * tok
    firsts = jnp.concatenate([first_of_mine, first_of_partner, my_index[None] * tok])
    keys_at = (firsts[:, None] + jnp.arange(tok, dtype=jnp.int32)[None, :]).reshape(1, -1)

    vmem = pl.BlockSpec(memory_space=pltpu.VMEM)
    hbm = pl.BlockSpec(memory_space=pl.ANY)
    scratch = [pltpu.VMEM((nx * nc * part, cols), bf), pltpu.SemaphoreType.DMA((nx * nc,))]
    queries = pl.pallas_call(
        queries_kernel,
        out_shape=jax.ShapeDtypeStruct((tok, cols), bf),
        in_specs=[vmem, vmem, vmem, hbm],
        out_specs=vmem,
        scratch_shapes=scratch,
        name="queries",
    )(reordered, cosine, sine, qo_all)
    reach_back = jnp.maximum(own_start, token_index - (WINDOW - 1))
    partial = pl.pallas_call(
        attend_kernel,
        out_shape=jax.ShapeDtypeStruct((nx, tok, shard), bf),
        in_specs=[vmem] * 7 + [hbm],
        out_specs=vmem,
        scratch_shapes=scratch,
        name="attend",
    )(queries, mine, partner, own_kv, keys_at, token_index[:, None], reach_back[:, None], qo_all)

    received = lax.all_to_all(partial, "tp", 0, 0, tiled=True)
    summed = jnp.zeros((tok, shard), jnp.float32)
    for g in range(nx):
        summed = summed + lax.dot_general(
            received[g], perm, (((1,), (1,)), ((), ())), preferred_element_type=jnp.float32
        )
    hidden = (tokens.astype(jnp.float32) + summed).astype(bf)
    return (hidden, kv_cache)


def solution(mesh):
    fine = Mesh(mesh.devices.reshape(*GRID, mesh.shape["tp"]), (*SEQ, "tp"))
    in_specs = (P(SEQ, "tp"), P(SEQ), P(), P(SEQ, "tp"), P(SEQ, None), P("tp", SEQ))
    out_specs = (P(SEQ, "tp"), P(SEQ, None))
    return jax.shard_map(per_device, mesh=fine, in_specs=in_specs, out_specs=out_specs, check_vma=False)
```

```python
import jax
import jax.numpy as jnp
from jax import lax
from jax.experimental import pallas as pl
from jax.experimental.pallas import tpu as pltpu
from jax.sharding import Mesh, PartitionSpec as P


HD = 256
WINDOW = 2048
SEGS = 32
GRID = (4, 2, 8, 2)
SEQ = ("x", "yh", "z", "c")


def rms_norm(values, gain):
    wide = values.astype(jnp.float32)
    scaled = wide * lax.rsqrt(jnp.mean(wide * wide, axis=-1, keepdims=True) + 1e-06)
    return (scaled * gain.astype(jnp.float32)).astype(jnp.bfloat16)


def angles(positions):
    quarter = HD // 4
    freq = 10000.0 ** (-jnp.arange(quarter, dtype=jnp.float32) / quarter)
    angle = positions[:, None] * freq
    cosine, sine = jnp.cos(angle), jnp.sin(angle)
    return jnp.concatenate([cosine, cosine], axis=1), jnp.concatenate([-sine, sine], axis=1)


def after(value, *others):
    return lax.optimization_barrier((value, *others))[0]


def spread(slab, axes, count):
    copies = jnp.broadcast_to(slab[None], (count, *slab.shape))
    return lax.all_to_all(copies, axes, 0, 0, tiled=True)


def in_order(shares, here):
    count = len(shares)
    ordered = []
    for g in range(count):
        came = (here - g) % count
        share = shares[count - 1]
        for k in range(count - 1):
            share = jnp.where(came == k, shares[k], share)
        ordered.append(share)
    return ordered


def natural_to_gathered(per, rows, slab, ny, core_first):
    nz = per // rows // ny // 2
    width = per // rows * slab
    nat = lax.broadcasted_iota(jnp.int32, (per, width), 0)
    gat = lax.broadcasted_iota(jnp.int32, (per, width), 1)
    place, row = gat // slab, gat % slab
    outer, z = place // nz, place % nz
    core, half = (outer // ny, outer % ny) if core_first else (outer % 2, outer // 2)
    source = ((half * nz + z) * 2 + core) * rows + row
    return ((nat == source) & (row < rows)).astype(jnp.bfloat16)


def turned(values, hot):
    per = hot.shape[0]
    return jnp.concatenate(
        [
            jnp.dot(values[:, g : g + per], hot, preferred_element_type=jnp.float32).astype(jnp.bfloat16)
            for g in range(0, values.shape[1], per)
        ],
        axis=1,
    )


def fetch(qo_ref, at, weights_ref, sems):
    groups = qo_ref.shape[0]
    part = qo_ref.shape[1] // 2
    copies = [
        pltpu.make_async_copy(
            qo_ref.at[g, pl.ds(at * part, part), :], weights_ref.at[pl.ds(g * part, part), :], sems.at[g]
        )
        for g in range(groups)
    ]
    for copy in copies:
        copy.start()
    return copies


def queries_kernel(normed_ref, cosine_ref, sine_ref, qo_ref, out_ref, weights_ref, sems):
    for copy in fetch(qo_ref, 0, weights_ref, sems):
        copy.wait()
    raw = jnp.dot(normed_ref[...], weights_ref[...], preferred_element_type=jnp.float32) * HD ** (-0.5)
    half = HD // 2
    for h in range(raw.shape[1] // HD):
        lo = raw[:, h * HD : h * HD + half]
        turned = lo * cosine_ref[...] + pltpu.roll(lo, half // 2, 1) * sine_ref[...]
        out_ref[:, h * HD : h * HD + half] = turned.astype(out_ref.dtype)
        out_ref[:, h * HD + half : (h + 1) * HD] = raw[:, h * HD + half : (h + 1) * HD].astype(
            out_ref.dtype
        )


def attend_kernel(
    queries_ref, mine_ref, partner_ref, own_ref, keys_at_ref, token_ref, first_ref, qo_ref, out_ref, weights_ref, sems
):
    copies = fetch(qo_ref, 1, weights_ref, sems)

    def whole(t):
        far = [ref[:, t].reshape(ref.shape[0] * ref.shape[2], ref.shape[3]) for ref in (mine_ref, partner_ref)]
        return jnp.concatenate([*far, own_ref[t]], axis=0)

    keys = jnp.concatenate([whole(0), whole(1)], axis=1)
    values = jnp.concatenate([whole(2), whole(3)], axis=1)
    at = keys_at_ref[...]
    live = (at <= token_ref[...]) & (at >= first_ref[...])
    heads = []
    for h in range(queries_ref.shape[1] // HD):
        scores = lax.dot_general(
            queries_ref[:, h * HD : (h + 1) * HD],
            keys,
            (((1,), (1,)), ((), ())),
            preferred_element_type=jnp.float32,
        )
        scores = jnp.where(live, scores, -1e30)
        powered = jnp.exp(scores - jnp.max(scores, axis=1, keepdims=True))
        weights = (powered * (1.0 / jnp.sum(powered, axis=1, keepdims=True))).astype(jnp.bfloat16)
        heads.append(
            jnp.dot(weights, values, preferred_element_type=jnp.float32).astype(jnp.bfloat16)
        )
    attended = jnp.concatenate(heads, axis=1)
    shard = out_ref.shape[2]
    for copy in copies:
        copy.wait()
    for g in range(out_ref.shape[0]):
        out_ref[g] = lax.dot_general(
            attended,
            weights_ref[g * shard : (g + 1) * shard, :],
            (((1,), (1,)), ((), ())),
            preferred_element_type=jnp.float32,
        ).astype(out_ref.dtype)


def per_device(tokens, seg_ids, norm_gain, w_query, w_keyval, w_out):
    nx, ny, nz, nc = GRID
    tok, shard = tokens.shape
    rows = w_query.shape[0]
    cols = w_query.shape[1]
    ix, iy, iz, ic = (lax.axis_index(a) for a in SEQ)
    it = lax.axis_index("tp")
    my_block = ix * ny + iy
    my_index = (my_block * nz + iz) * nc + ic
    bf = jnp.bfloat16
    both = [(0, 1), (1, 0)]

    share = 2 * HD // nx
    slab = rows + 4
    ids = jnp.pad(seg_ids.astype(bf)[None, :], ((0, 31 - rows), (0, 0)))
    chosen = w_keyval[:, (nx - 1) * share :]
    for t in range(nx - 1):
        chosen = jnp.where(it == t, w_keyval[:, t * share : (t + 1) * share], chosen)
    kv_slab = jnp.concatenate([chosen, ids], axis=0)
    folded = jnp.concatenate([kv_slab[i : i + 8] for i in range(0, 32, 8)], axis=1)
    near = spread(jnp.concatenate([w_query, w_out.T, folded], axis=0), "z", nz)

    others = [lax.ppermute(tokens, "tp", [(i, (i + k) % nx) for i in range(nx)]) for k in range(1, nx)]

    kv_near = jnp.concatenate(
        [near[:, 2 * rows :, i * share : (i + 1) * share] for i in range(slab // 8)], axis=1
    )
    kv_mine = spread(kv_near, ("x", "yh"), nx * ny)
    kv_twin = lax.ppermute(kv_mine, "c", both)
    part = nz * rows
    qo_send = jnp.concatenate(
        [near[:, :rows].reshape(part, cols), near[:, rows : 2 * rows].reshape(part, cols)], axis=0
    )
    qo_all = lax.all_gather(qo_send, ("x", "yh", "c"), axis=0, tiled=False)

    normed = rms_norm(jnp.concatenate(in_order([tokens, *others], it), axis=1), norm_gain)
    padded = turned(normed, natural_to_gathered(shard, rows, slab, ny, True))
    half = ny * nz * slab
    of_core = [
        jnp.concatenate([padded[:, i * half : (i + 1) * half] for i in range(c, nx * nc, nc)], axis=1)
        for c in range(nc)
    ]
    for_mine = jnp.where(ic == 0, of_core[0], of_core[1])
    for_twin = jnp.where(ic == 0, of_core[1], of_core[0])
    kv_mine, for_mine, for_twin = lax.optimization_barrier((kv_mine, for_mine, for_twin))

    all_ids = jnp.concatenate([kv_mine[:, :, rows], kv_twin[:, :, rows]], axis=0).astype(jnp.int32)
    labels = jnp.arange(SEGS, dtype=jnp.int32)
    starts = jnp.sum((all_ids.reshape(-1)[None, :] < labels[:, None]).astype(jnp.int32), axis=1)
    own_start = jnp.sum(jnp.where(seg_ids[:, None] == labels[None, :], starts[None, :], 0), axis=1)
    token_index = my_index * tok + jnp.arange(tok, dtype=jnp.int32)
    cosine, sine = angles((token_index - own_start).astype(jnp.float32))

    kv_raw = jnp.dot(
        for_mine, kv_mine.reshape(nx * half, share), preferred_element_type=jnp.float32
    ) + jnp.dot(for_twin, kv_twin.reshape(nx * half, share), preferred_element_type=jnp.float32)
    quarter = HD // 4
    swapped = jnp.concatenate([kv_raw[:, quarter:], kv_raw[:, :quarter]], axis=1)
    kv_share = jnp.where(it == 0, kv_raw * cosine + swapped * sine, kv_raw).astype(bf)

    block = nz * nc
    devices = nx * ny * block
    before = lax.ppermute(kv_share, SEQ, [(i, i + block) for i in range(devices - block)])
    chips = jnp.arange(nz, dtype=jnp.int32)
    to_send = jnp.where((chips > iz)[:, None, None], kv_share[None], before[None])
    to_send = jnp.broadcast_to(to_send[:, None], (nz, nx, tok, share)).reshape(nz * nx, tok, share)
    mine = lax.all_to_all(to_send, ("z", "tp"), 0, 0, tiled=True).reshape(nz, nx, tok, share)
    rest = [lax.ppermute(kv_share, "tp", [(i, (i + k) % nx) for i in range(nx)]) for k in range(1, nx)]
    own_kv = jnp.stack(in_order([kv_share, *rest], it))
    kv_cache = jnp.concatenate(list(own_kv), axis=1)
    at_self = (chips == iz)[:, None, None, None] & (ic == 0)
    partner = lax.ppermute(jnp.where(at_self, own_kv[None], mine), "c", both)
    perm = natural_to_gathered(shard, rows, rows, ny, False)
    reordered = turned(after(normed, to_send), perm)
    block_of_mine = my_block - (chips >= iz).astype(jnp.int32)
    block_of_partner = my_block - jnp.where(ic == 1, chips > iz, chips >= iz).astype(jnp.int32)
    first_of_mine = ((block_of_mine * nz + chips) * nc + ic) * tok
    first_of_partner = ((block_of_partner * nz + chips) * nc + 1 - ic) * tok
    firsts = jnp.concatenate([first_of_mine, first_of_partner, my_index[None] * tok])
    keys_at = (firsts[:, None] + jnp.arange(tok, dtype=jnp.int32)[None, :]).reshape(1, -1)

    vmem = pl.BlockSpec(memory_space=pltpu.VMEM)
    hbm = pl.BlockSpec(memory_space=pl.ANY)
    scratch = [pltpu.VMEM((nx * shard, cols), bf), pltpu.SemaphoreType.DMA((nx * ny * nc,))]
    queries = pl.pallas_call(
        queries_kernel,
        out_shape=jax.ShapeDtypeStruct((tok, cols), bf),
        in_specs=[vmem, vmem, vmem, hbm],
        out_specs=vmem,
        scratch_shapes=scratch,
        name="queries",
    )(reordered, cosine, sine, qo_all)
    reach_back = jnp.maximum(own_start, token_index - (WINDOW - 1))
    partial = pl.pallas_call(
        attend_kernel,
        out_shape=jax.ShapeDtypeStruct((nx, tok, shard), bf),
        in_specs=[vmem] * 7 + [hbm],
        out_specs=vmem,
        scratch_shapes=scratch,
        name="attend",
    )(queries, mine, partner, own_kv, keys_at, token_index[:, None], reach_back[:, None], qo_all)

    received = lax.all_to_all(partial, "tp", 0, 0, tiled=True)
    summed = jnp.zeros((tok, shard), jnp.float32)
    for g in range(nx):
        summed = summed + lax.dot_general(
            received[g], perm, (((1,), (1,)), ((), ())), preferred_element_type=jnp.float32
        )
    hidden = (tokens.astype(jnp.float32) + summed).astype(bf)
    return (hidden, kv_cache)


def solution(mesh):
    fine = Mesh(mesh.devices.reshape(*GRID, mesh.shape["tp"]), (*SEQ, "tp"))
    in_specs = (P(SEQ, "tp"), P(SEQ), P(), P(SEQ, "tp"), P(SEQ, None), P("tp", SEQ))
    out_specs = (P(SEQ, "tp"), P(SEQ, None))
    return jax.shard_map(per_device, mesh=fine, in_specs=in_specs, out_specs=out_specs, check_vma=False)
```

```python
import jax
import jax.numpy as jnp
from jax import lax
from jax.experimental import pallas as pl
from jax.experimental.pallas import tpu as pltpu
from jax.sharding import Mesh, PartitionSpec as P


HD = 256
WINDOW = 2048
SEGS = 32
GRID = (4, 2, 8, 2)
SEQ = ("x", "yh", "z", "c")


def rms_norm(values, gain):
    wide = values.astype(jnp.float32)
    scaled = wide * lax.rsqrt(jnp.mean(wide * wide, axis=-1, keepdims=True) + 1e-06)
    return (scaled * gain.astype(jnp.float32)).astype(jnp.bfloat16)


def angles(positions):
    quarter = HD // 4
    freq = 10000.0 ** (-jnp.arange(quarter, dtype=jnp.float32) / quarter)
    angle = positions[:, None] * freq
    cosine, sine = jnp.cos(angle), jnp.sin(angle)
    return jnp.concatenate([cosine, cosine], axis=1), jnp.concatenate([-sine, sine], axis=1)


def after(value, *others):
    return lax.optimization_barrier((value, *others))[0]


def spread(slab, axes, count):
    copies = jnp.broadcast_to(slab[None], (count, *slab.shape))
    return lax.all_to_all(copies, axes, 0, 0, tiled=True)


def in_order(shares, here):
    count = len(shares)
    ordered = []
    for g in range(count):
        came = (here - g) % count
        share = shares[count - 1]
        for k in range(count - 1):
            share = jnp.where(came == k, shares[k], share)
        ordered.append(share)
    return ordered


def natural_to_gathered(per, rows, slab, ny, z_first):
    nz = per // rows // ny // 2
    width = per // rows * slab
    nat = lax.broadcasted_iota(jnp.int32, (per, width), 0)
    gat = lax.broadcasted_iota(jnp.int32, (per, width), 1)
    place, row = gat // slab, gat % slab
    core, rest = place // (ny * nz), place % (ny * nz)
    z, half = (rest // ny, rest % ny) if z_first else (rest % nz, rest // nz)
    source = ((half * nz + z) * 2 + core) * rows + row
    return ((nat == source) & (row < rows)).astype(jnp.bfloat16)


def turned(values, hot):
    per = hot.shape[0]
    return jnp.concatenate(
        [
            jnp.dot(values[:, g : g + per], hot, preferred_element_type=jnp.float32).astype(jnp.bfloat16)
            for g in range(0, values.shape[1], per)
        ],
        axis=1,
    )


def fetch(qo_ref, at, weights_ref, sems):
    groups = qo_ref.shape[0]
    part = qo_ref.shape[1] // 2
    copies = [
        pltpu.make_async_copy(
            qo_ref.at[g, pl.ds(at * part, part), :], weights_ref.at[pl.ds(g * part, part), :], sems.at[g]
        )
        for g in range(groups)
    ]
    for copy in copies:
        copy.start()
    return copies


def queries_kernel(normed_ref, cosine_ref, sine_ref, qo_ref, out_ref, weights_ref, sems):
    for copy in fetch(qo_ref, 0, weights_ref, sems):
        copy.wait()
    raw = jnp.dot(normed_ref[...], weights_ref[...], preferred_element_type=jnp.float32) * HD ** (-0.5)
    half = HD // 2
    for h in range(raw.shape[1] // HD):
        lo = raw[:, h * HD : h * HD + half]
        turned = lo * cosine_ref[...] + pltpu.roll(lo, half // 2, 1) * sine_ref[...]
        out_ref[:, h * HD : h * HD + half] = turned.astype(out_ref.dtype)
        out_ref[:, h * HD + half : (h + 1) * HD] = raw[:, h * HD + half : (h + 1) * HD].astype(
            out_ref.dtype
        )


def attend_kernel(
    queries_ref, mine_ref, partner_ref, own_ref, keys_at_ref, token_ref, first_ref, qo_ref, out_ref, weights_ref, sems
):
    copies = fetch(qo_ref, 1, weights_ref, sems)

    def whole(t):
        far = [ref[:, t].reshape(ref.shape[0] * ref.shape[2], ref.shape[3]) for ref in (mine_ref, partner_ref)]
        return jnp.concatenate([*far, own_ref[t]], axis=0)

    keys = jnp.concatenate([whole(0), whole(1)], axis=1)
    values = jnp.concatenate([whole(2), whole(3)], axis=1)
    at = keys_at_ref[...]
    live = (at <= token_ref[...]) & (at >= first_ref[...])
    heads = []
    for h in range(queries_ref.shape[1] // HD):
        scores = lax.dot_general(
            queries_ref[:, h * HD : (h + 1) * HD],
            keys,
            (((1,), (1,)), ((), ())),
            preferred_element_type=jnp.float32,
        )
        scores = jnp.where(live, scores, -1e30)
        powered = jnp.exp(scores - jnp.max(scores, axis=1, keepdims=True))
        weights = (powered * (1.0 / jnp.sum(powered, axis=1, keepdims=True))).astype(jnp.bfloat16)
        heads.append(
            jnp.dot(weights, values, preferred_element_type=jnp.float32).astype(jnp.bfloat16)
        )
    attended = jnp.concatenate(heads, axis=1)
    shard = out_ref.shape[2]
    for copy in copies:
        copy.wait()
    for g in range(out_ref.shape[0]):
        out_ref[g] = lax.dot_general(
            attended,
            weights_ref[g * shard : (g + 1) * shard, :],
            (((1,), (1,)), ((), ())),
            preferred_element_type=jnp.float32,
        ).astype(out_ref.dtype)


def per_device(tokens, seg_ids, norm_gain, w_query, w_keyval, w_out):
    nx, ny, nz, nc = GRID
    tok, shard = tokens.shape
    rows = w_query.shape[0]
    cols = w_query.shape[1]
    ix, iy, iz, ic = (lax.axis_index(a) for a in SEQ)
    it = lax.axis_index("tp")
    my_block = ix * ny + iy
    my_index = (my_block * nz + iz) * nc + ic
    bf = jnp.bfloat16
    both = [(0, 1), (1, 0)]

    share = 2 * HD // nx
    slab = rows + 4
    ids = jnp.pad(seg_ids.astype(bf)[None, :], ((0, 31 - rows), (0, 0)))
    chosen = w_keyval[:, (nx - 1) * share :]
    for t in range(nx - 1):
        chosen = jnp.where(it == t, w_keyval[:, t * share : (t + 1) * share], chosen)
    kv_slab = jnp.concatenate([chosen, ids], axis=0)
    folded = jnp.concatenate([kv_slab[i : i + 8] for i in range(0, 32, 8)], axis=1)
    near = spread(folded, "z", nz)
    kv_near = jnp.concatenate([near[:, :, i * share : (i + 1) * share] for i in range(slab // 8)], axis=1)
    kv_mine = spread(kv_near, ("x", "yh"), nx * ny)
    kv_twin = lax.ppermute(kv_mine, "c", both)

    others = [lax.ppermute(tokens, "tp", [(i, (i + k) % nx) for i in range(nx)]) for k in range(1, nx)]

    qo_own = jnp.concatenate([w_query, w_out.T], axis=0)
    qo_other = lax.ppermute(qo_own, "yh", both)
    low = jnp.where(iy == 0, qo_own, qo_other)
    high = jnp.where(iy == 0, qo_other, qo_own)
    qo_pair = jnp.concatenate([low[:rows], high[:rows], low[rows:], high[rows:]], axis=0)
    qo_near = spread(after(qo_pair, kv_mine), "z", nz)
    part = nz * ny * rows
    qo_send = jnp.concatenate(
        [qo_near[:, : ny * rows].reshape(part, cols), qo_near[:, ny * rows :].reshape(part, cols)], axis=0
    )
    qo_all = lax.all_gather(qo_send, ("x", "c"), axis=0, tiled=False)

    normed = rms_norm(jnp.concatenate(in_order([tokens, *others], it), axis=1), norm_gain)
    padded = turned(normed, natural_to_gathered(shard, rows, slab, ny, False))
    half = ny * nz * slab
    of_core = [
        jnp.concatenate([padded[:, i * half : (i + 1) * half] for i in range(c, nx * nc, nc)], axis=1)
        for c in range(nc)
    ]
    for_mine = jnp.where(ic == 0, of_core[0], of_core[1])
    for_twin = jnp.where(ic == 0, of_core[1], of_core[0])
    kv_mine, for_mine, for_twin = lax.optimization_barrier((kv_mine, for_mine, for_twin))

    all_ids = jnp.concatenate([kv_mine[:, :, rows], kv_twin[:, :, rows]], axis=0).astype(jnp.int32)
    labels = jnp.arange(SEGS, dtype=jnp.int32)
    starts = jnp.sum((all_ids.reshape(-1)[None, :] < labels[:, None]).astype(jnp.int32), axis=1)
    own_start = jnp.sum(jnp.where(seg_ids[:, None] == labels[None, :], starts[None, :], 0), axis=1)
    token_index = my_index * tok + jnp.arange(tok, dtype=jnp.int32)
    cosine, sine = angles((token_index - own_start).astype(jnp.float32))

    kv_raw = jnp.dot(
        for_mine, kv_mine.reshape(nx * half, share), preferred_element_type=jnp.float32
    ) + jnp.dot(for_twin, kv_twin.reshape(nx * half, share), preferred_element_type=jnp.float32)
    quarter = HD // 4
    swapped = jnp.concatenate([kv_raw[:, quarter:], kv_raw[:, :quarter]], axis=1)
    kv_share = jnp.where(it == 0, kv_raw * cosine + swapped * sine, kv_raw).astype(bf)

    block = nz * nc
    devices = nx * ny * block
    before = lax.ppermute(kv_share, SEQ, [(i, i + block) for i in range(devices - block)])
    chips = jnp.arange(nz, dtype=jnp.int32)
    to_send = jnp.where((chips > iz)[:, None, None], kv_share[None], before[None])
    to_send = after(to_send, qo_send)
    to_send = jnp.broadcast_to(to_send[:, None], (nz, nx, tok, share)).reshape(nz * nx, tok, share)
    mine = lax.all_to_all(to_send, ("z", "tp"), 0, 0, tiled=True).reshape(nz, nx, tok, share)
    rest = [lax.ppermute(kv_share, "tp", [(i, (i + k) % nx) for i in range(nx)]) for k in range(1, nx)]
    own_kv = jnp.stack(in_order([kv_share, *rest], it))
    kv_cache = jnp.concatenate(list(own_kv), axis=1)
    at_self = (chips == iz)[:, None, None, None] & (ic == 0)
    partner = lax.ppermute(jnp.where(at_self, own_kv[None], mine), "c", both)
    perm = natural_to_gathered(shard, rows, rows, ny, True)
    reordered = turned(after(normed, to_send), perm)
    block_of_mine = my_block - (chips >= iz).astype(jnp.int32)
    block_of_partner = my_block - jnp.where(ic == 1, chips > iz, chips >= iz).astype(jnp.int32)
    first_of_mine = ((block_of_mine * nz + chips) * nc + ic) * tok
    first_of_partner = ((block_of_partner * nz + chips) * nc + 1 - ic) * tok
    firsts = jnp.concatenate([first_of_mine, first_of_partner, my_index[None] * tok])
    keys_at = (firsts[:, None] + jnp.arange(tok, dtype=jnp.int32)[None, :]).reshape(1, -1)

    vmem = pl.BlockSpec(memory_space=pltpu.VMEM)
    hbm = pl.BlockSpec(memory_space=pl.ANY)
    scratch = [pltpu.VMEM((nx * shard, cols), bf), pltpu.SemaphoreType.DMA((nx * nc,))]
    queries = pl.pallas_call(
        queries_kernel,
        out_shape=jax.ShapeDtypeStruct((tok, cols), bf),
        in_specs=[vmem, vmem, vmem, hbm],
        out_specs=vmem,
        scratch_shapes=scratch,
        name="queries",
    )(reordered, cosine, sine, qo_all)
    reach_back = jnp.maximum(own_start, token_index - (WINDOW - 1))
    partial = pl.pallas_call(
        attend_kernel,
        out_shape=jax.ShapeDtypeStruct((nx, tok, shard), bf),
        in_specs=[vmem] * 7 + [hbm],
        out_specs=vmem,
        scratch_shapes=scratch,
        name="attend",
    )(queries, mine, partner, own_kv, keys_at, token_index[:, None], reach_back[:, None], qo_all)

    received = lax.all_to_all(partial, "tp", 0, 0, tiled=True)
    summed = jnp.zeros((tok, shard), jnp.float32)
    for g in range(nx):
        summed = summed + lax.dot_general(
            received[g], perm, (((1,), (1,)), ((), ())), preferred_element_type=jnp.float32
        )
    hidden = (tokens.astype(jnp.float32) + summed).astype(bf)
    return (hidden, kv_cache)


def solution(mesh):
    fine = Mesh(mesh.devices.reshape(*GRID, mesh.shape["tp"]), (*SEQ, "tp"))
    in_specs = (P(SEQ, "tp"), P(SEQ), P(), P(SEQ, "tp"), P(SEQ, None), P("tp", SEQ))
    out_specs = (P(SEQ, "tp"), P(SEQ, None))
    return jax.shard_map(per_device, mesh=fine, in_specs=in_specs, out_specs=out_specs, check_vma=False)
```

```python
import jax
import jax.numpy as jnp
from jax import lax
from jax.experimental import pallas as pl
from jax.experimental.pallas import tpu as pltpu
from jax.sharding import Mesh, PartitionSpec as P


HD = 256
WINDOW = 2048
SEGS = 32
GRID = (4, 2, 8, 2)
SEQ = ("x", "yh", "z", "c")


def rms_norm(values, gain):
    wide = values.astype(jnp.float32)
    scaled = wide * lax.rsqrt(jnp.mean(wide * wide, axis=-1, keepdims=True) + 1e-06)
    return (scaled * gain.astype(jnp.float32)).astype(jnp.bfloat16)


def angles(positions):
    quarter = HD // 4
    freq = 10000.0 ** (-jnp.arange(quarter, dtype=jnp.float32) / quarter)
    angle = positions[:, None] * freq
    cosine, sine = jnp.cos(angle), jnp.sin(angle)
    return jnp.concatenate([cosine, cosine], axis=1), jnp.concatenate([-sine, sine], axis=1)


def after(value, *others):
    return lax.optimization_barrier((value, *others))[0]


def spread(slab, axes, count):
    copies = jnp.broadcast_to(slab[None], (count, *slab.shape))
    return lax.all_to_all(copies, axes, 0, 0, tiled=True)


def in_order(shares, here):
    count = len(shares)
    ordered = []
    for g in range(count):
        came = (here - g) % count
        share = shares[count - 1]
        for k in range(count - 1):
            share = jnp.where(came == k, shares[k], share)
        ordered.append(share)
    return ordered


def natural_to_gathered(per, rows, slab):
    width = per // rows * slab
    nat = lax.broadcasted_iota(jnp.int32, (per, width), 0)
    gat = lax.broadcasted_iota(jnp.int32, (per, width), 1)
    half = width // 2
    core, rest = gat // half, gat % half
    place, row = rest // slab, rest % slab
    source = (place * 2 + core) * rows + row
    return ((nat == source) & (row < rows)).astype(jnp.bfloat16)


def turned(values, hot):
    per = hot.shape[0]
    return jnp.concatenate(
        [
            jnp.dot(values[:, g : g + per], hot, preferred_element_type=jnp.float32).astype(jnp.bfloat16)
            for g in range(0, values.shape[1], per)
        ],
        axis=1,
    )


def fetch(qo_ref, at, weights_ref, sems):
    groups = qo_ref.shape[0]
    part = qo_ref.shape[1] // 2
    copies = [
        pltpu.make_async_copy(
            qo_ref.at[g, pl.ds(at * part, part), :], weights_ref.at[pl.ds(g * part, part), :], sems.at[g]
        )
        for g in range(groups)
    ]
    for copy in copies:
        copy.start()
    return copies


def queries_kernel(normed_ref, cosine_ref, sine_ref, qo_ref, out_ref, weights_ref, sems):
    for copy in fetch(qo_ref, 0, weights_ref, sems):
        copy.wait()
    raw = jnp.dot(normed_ref[...], weights_ref[...], preferred_element_type=jnp.float32) * HD ** (-0.5)
    half = HD // 2
    for h in range(raw.shape[1] // HD):
        lo = raw[:, h * HD : h * HD + half]
        turned = lo * cosine_ref[...] + pltpu.roll(lo, half // 2, 1) * sine_ref[...]
        out_ref[:, h * HD : h * HD + half] = turned.astype(out_ref.dtype)
        out_ref[:, h * HD + half : (h + 1) * HD] = raw[:, h * HD + half : (h + 1) * HD].astype(
            out_ref.dtype
        )


def attend_kernel(
    queries_ref, mine_ref, partner_ref, own_ref, keys_at_ref, token_ref, first_ref, qo_ref, out_ref, weights_ref, sems
):
    copies = fetch(qo_ref, 1, weights_ref, sems)

    def whole(t):
        far = [ref[:, t].reshape(ref.shape[0] * ref.shape[2], ref.shape[3]) for ref in (mine_ref, partner_ref)]
        return jnp.concatenate([*far, own_ref[t]], axis=0)

    keys = jnp.concatenate([whole(0), whole(1)], axis=1)
    values = jnp.concatenate([whole(2), whole(3)], axis=1)
    at = keys_at_ref[...]
    live = (at <= token_ref[...]) & (at >= first_ref[...])
    heads = []
    for h in range(queries_ref.shape[1] // HD):
        scores = lax.dot_general(
            queries_ref[:, h * HD : (h + 1) * HD],
            keys,
            (((1,), (1,)), ((), ())),
            preferred_element_type=jnp.float32,
        )
        scores = jnp.where(live, scores, -1e30)
        powered = jnp.exp(scores - jnp.max(scores, axis=1, keepdims=True))
        weights = (powered * (1.0 / jnp.sum(powered, axis=1, keepdims=True))).astype(jnp.bfloat16)
        heads.append(
            jnp.dot(weights, values, preferred_element_type=jnp.float32).astype(jnp.bfloat16)
        )
    attended = jnp.concatenate(heads, axis=1)
    shard = out_ref.shape[2]
    for copy in copies:
        copy.wait()
    for g in range(out_ref.shape[0]):
        out_ref[g] = lax.dot_general(
            attended,
            weights_ref[g * shard : (g + 1) * shard, :],
            (((1,), (1,)), ((), ())),
            preferred_element_type=jnp.float32,
        ).astype(out_ref.dtype)


def per_device(tokens, seg_ids, norm_gain, w_query, w_keyval, w_out):
    nx, ny, nz, nc = GRID
    tok, shard = tokens.shape
    rows = w_query.shape[0]
    cols = w_query.shape[1]
    ix, iy, iz, ic = (lax.axis_index(a) for a in SEQ)
    it = lax.axis_index("tp")
    my_block = ix * ny + iy
    my_index = (my_block * nz + iz) * nc + ic
    bf = jnp.bfloat16
    both = [(0, 1), (1, 0)]

    share = 2 * HD // nx
    slab = rows + 4
    ids = jnp.pad(seg_ids.astype(bf)[None, :], ((0, 31 - rows), (0, 0)))
    chosen = w_keyval[:, (nx - 1) * share :]
    for t in range(nx - 1):
        chosen = jnp.where(it == t, w_keyval[:, t * share : (t + 1) * share], chosen)
    kv_slab = jnp.concatenate([chosen, ids], axis=0)
    folded = jnp.concatenate([kv_slab[i : i + 8] for i in range(0, 32, 8)], axis=1)
    near = spread(jnp.concatenate([w_query, w_out.T, folded], axis=0), ("yh", "z"), ny * nz)

    others = [lax.ppermute(tokens, "tp", [(i, (i + k) % nx) for i in range(nx)]) for k in range(1, nx)]

    kv_near = jnp.concatenate(
        [near[:, 2 * rows :, i * share : (i + 1) * share] for i in range(slab // 8)], axis=1
    )
    kv_all = spread(kv_near, ("x", "c"), nx * nc)
    part = nz * ny * rows
    qo_send = jnp.concatenate(
        [near[:, :rows].reshape(part, cols), near[:, rows : 2 * rows].reshape(part, cols)], axis=0
    )
    qo_all = lax.all_gather(qo_send, ("x", "c"), axis=0, tiled=False)

    groups = in_order([tokens, *others], it)
    normed = rms_norm(jnp.concatenate(groups, axis=1), norm_gain)
    padded = turned(normed, natural_to_gathered(shard, rows, slab))
    kv_all, padded = lax.optimization_barrier((kv_all, padded))

    all_ids = kv_all[:, :, rows].astype(jnp.int32)
    labels = jnp.arange(SEGS, dtype=jnp.int32)
    starts = jnp.sum((all_ids.reshape(-1)[None, :] < labels[:, None]).astype(jnp.int32), axis=1)
    own_start = jnp.sum(jnp.where(seg_ids[:, None] == labels[None, :], starts[None, :], 0), axis=1)
    token_index = my_index * tok + jnp.arange(tok, dtype=jnp.int32)
    cosine, sine = angles((token_index - own_start).astype(jnp.float32))

    kv_raw = jnp.dot(
        padded, kv_all.reshape(nx * nc * ny * nz * slab, share), preferred_element_type=jnp.float32
    )
    quarter = HD // 4
    swapped = jnp.concatenate([kv_raw[:, quarter:], kv_raw[:, :quarter]], axis=1)
    kv_share = jnp.where(it == 0, kv_raw * cosine + swapped * sine, kv_raw).astype(bf)

    block = nz * nc
    devices = nx * ny * block
    before = lax.ppermute(kv_share, SEQ, [(i, i + block) for i in range(devices - block)])
    chips = jnp.arange(nz, dtype=jnp.int32)
    to_send = jnp.where((chips > iz)[:, None, None], kv_share[None], before[None])
    to_send = jnp.broadcast_to(to_send[:, None], (nz, nx, tok, share)).reshape(nz * nx, tok, share)
    mine = lax.all_to_all(to_send, ("z", "tp"), 0, 0, tiled=True).reshape(nz, nx, tok, share)
    rest = [lax.ppermute(kv_share, "tp", [(i, (i + k) % nx) for i in range(nx)]) for k in range(1, nx)]
    own_kv = jnp.stack(in_order([kv_share, *rest], it))
    kv_cache = jnp.concatenate(list(own_kv), axis=1)
    at_self = (chips == iz)[:, None, None, None] & (ic == 0)
    partner = lax.ppermute(jnp.where(at_self, own_kv[None], mine), "c", both)
    perm = natural_to_gathered(shard, rows, rows)
    reordered = turned(after(normed, to_send), perm)
    block_of_mine = my_block - (chips >= iz).astype(jnp.int32)
    block_of_partner = my_block - jnp.where(ic == 1, chips > iz, chips >= iz).astype(jnp.int32)
    first_of_mine = ((block_of_mine * nz + chips) * nc + ic) * tok
    first_of_partner = ((block_of_partner * nz + chips) * nc + 1 - ic) * tok
    firsts = jnp.concatenate([first_of_mine, first_of_partner, my_index[None] * tok])
    keys_at = (firsts[:, None] + jnp.arange(tok, dtype=jnp.int32)[None, :]).reshape(1, -1)

    vmem = pl.BlockSpec(memory_space=pltpu.VMEM)
    hbm = pl.BlockSpec(memory_space=pl.ANY)
    scratch = [pltpu.VMEM((nx * nc * part, cols), bf), pltpu.SemaphoreType.DMA((nx * nc,))]
    queries = pl.pallas_call(
        queries_kernel,
        out_shape=jax.ShapeDtypeStruct((tok, cols), bf),
        in_specs=[vmem, vmem, vmem, hbm],
        out_specs=vmem,
        scratch_shapes=scratch,
        name="queries",
    )(reordered, cosine, sine, qo_all)
    reach_back = jnp.maximum(own_start, token_index - (WINDOW - 1))
    partial = pl.pallas_call(
        attend_kernel,
        out_shape=jax.ShapeDtypeStruct((nx, tok, shard), bf),
        in_specs=[vmem] * 7 + [hbm],
        out_specs=vmem,
        scratch_shapes=scratch,
        name="attend",
    )(queries, mine, partner, own_kv, keys_at, token_index[:, None], reach_back[:, None], qo_all)

    received = lax.all_to_all(partial, "tp", 0, 0, tiled=True)
    summed = jnp.zeros((tok, shard), jnp.float32)
    for g in range(nx):
        summed = summed + lax.dot_general(
            received[g], perm, (((1,), (1,)), ((), ())), preferred_element_type=jnp.float32
        )
    hidden = (tokens.astype(jnp.float32) + summed).astype(bf)
    return (hidden, kv_cache)


def solution(mesh):
    fine = Mesh(mesh.devices.reshape(*GRID, mesh.shape["tp"]), (*SEQ, "tp"))
    in_specs = (P(SEQ, "tp"), P(SEQ), P(), P(SEQ, "tp"), P(SEQ, None), P("tp", SEQ))
    out_specs = (P(SEQ, "tp"), P(SEQ, None))
    return jax.shard_map(per_device, mesh=fine, in_specs=in_specs, out_specs=out_specs, check_vma=False)
```

```python
import jax
import jax.numpy as jnp
from jax import lax
from jax.experimental import pallas as pl
from jax.experimental.pallas import tpu as pltpu
from jax.sharding import Mesh, PartitionSpec as P


HD = 256
WINDOW = 2048
SEGS = 32
GRID = (4, 2, 8, 2)
SEQ = ("x", "yh", "z", "c")


def rms_norm(values, gain):
    wide = values.astype(jnp.float32)
    scaled = wide * lax.rsqrt(jnp.mean(wide * wide, axis=-1, keepdims=True) + 1e-06)
    return (scaled * gain.astype(jnp.float32)).astype(jnp.bfloat16)


def angles(positions):
    quarter = HD // 4
    freq = 10000.0 ** (-jnp.arange(quarter, dtype=jnp.float32) / quarter)
    angle = positions[:, None] * freq
    cosine, sine = jnp.cos(angle), jnp.sin(angle)
    return jnp.concatenate([cosine, cosine], axis=1), jnp.concatenate([-sine, sine], axis=1)


def after(value, *others):
    return lax.optimization_barrier((value, *others))[0]


def spread(slab, axes, count):
    copies = jnp.broadcast_to(slab[None], (count, *slab.shape))
    return lax.all_to_all(copies, axes, 0, 0, tiled=True)


def in_order(shares, here):
    count = len(shares)
    ordered = []
    for g in range(count):
        came = (here - g) % count
        share = shares[count - 1]
        for k in range(count - 1):
            share = jnp.where(came == k, shares[k], share)
        ordered.append(share)
    return ordered


def natural_to_gathered(per, rows, slab):
    width = per // rows * slab
    nat = lax.broadcasted_iota(jnp.int32, (per, width), 0)
    gat = lax.broadcasted_iota(jnp.int32, (per, width), 1)
    half = width // 2
    core, rest = gat // half, gat % half
    place, row = rest // slab, rest % slab
    source = (place * 2 + core) * rows + row
    return ((nat == source) & (row < rows)).astype(jnp.bfloat16)


def turned(values, hot):
    per = hot.shape[0]
    return jnp.concatenate(
        [
            jnp.dot(values[:, g : g + per], hot, preferred_element_type=jnp.float32).astype(jnp.bfloat16)
            for g in range(0, values.shape[1], per)
        ],
        axis=1,
    )


def fetch(qo_ref, at, weights_ref, sems):
    groups = qo_ref.shape[0]
    part = qo_ref.shape[1] // 2
    copies = [
        pltpu.make_async_copy(
            qo_ref.at[g, pl.ds(at * part, part), :], weights_ref.at[pl.ds(g * part, part), :], sems.at[g]
        )
        for g in range(groups)
    ]
    for copy in copies:
        copy.start()
    return copies


def queries_kernel(normed_ref, cosine_ref, sine_ref, qo_ref, out_ref, weights_ref, sems):
    for copy in fetch(qo_ref, 0, weights_ref, sems):
        copy.wait()
    raw = jnp.dot(normed_ref[...], weights_ref[...], preferred_element_type=jnp.float32) * HD ** (-0.5)
    half = HD // 2
    for h in range(raw.shape[1] // HD):
        lo = raw[:, h * HD : h * HD + half]
        turned = lo * cosine_ref[...] + pltpu.roll(lo, half // 2, 1) * sine_ref[...]
        out_ref[:, h * HD : h * HD + half] = turned.astype(out_ref.dtype)
        out_ref[:, h * HD + half : (h + 1) * HD] = raw[:, h * HD + half : (h + 1) * HD].astype(
            out_ref.dtype
        )


def attend_kernel(
    queries_ref, mine_ref, partner_ref, own_ref, keys_at_ref, token_ref, first_ref, qo_ref, out_ref, weights_ref, sems
):
    copies = fetch(qo_ref, 1, weights_ref, sems)

    def whole(t):
        far = [ref[:, t].reshape(ref.shape[0] * ref.shape[2], ref.shape[3]) for ref in (mine_ref, partner_ref)]
        return jnp.concatenate([*far, own_ref[t]], axis=0)

    keys = jnp.concatenate([whole(0), whole(1)], axis=1)
    values = jnp.concatenate([whole(2), whole(3)], axis=1)
    at = keys_at_ref[...]
    live = (at <= token_ref[...]) & (at >= first_ref[...])
    heads = []
    for h in range(queries_ref.shape[1] // HD):
        scores = lax.dot_general(
            queries_ref[:, h * HD : (h + 1) * HD],
            keys,
            (((1,), (1,)), ((), ())),
            preferred_element_type=jnp.float32,
        )
        scores = jnp.where(live, scores, -1e30)
        powered = jnp.exp(scores - jnp.max(scores, axis=1, keepdims=True))
        weights = (powered * (1.0 / jnp.sum(powered, axis=1, keepdims=True))).astype(jnp.bfloat16)
        heads.append(
            jnp.dot(weights, values, preferred_element_type=jnp.float32).astype(jnp.bfloat16)
        )
    attended = jnp.concatenate(heads, axis=1)
    shard = out_ref.shape[2]
    for copy in copies:
        copy.wait()
    for g in range(out_ref.shape[0]):
        out_ref[g] = lax.dot_general(
            attended,
            weights_ref[g * shard : (g + 1) * shard, :],
            (((1,), (1,)), ((), ())),
            preferred_element_type=jnp.float32,
        ).astype(out_ref.dtype)


def per_device(tokens, seg_ids, norm_gain, w_query, w_keyval, w_out):
    nx, ny, nz, nc = GRID
    tok, shard = tokens.shape
    rows = w_query.shape[0]
    cols = w_query.shape[1]
    ix, iy, iz, ic = (lax.axis_index(a) for a in SEQ)
    it = lax.axis_index("tp")
    my_block = ix * ny + iy
    my_index = (my_block * nz + iz) * nc + ic
    bf = jnp.bfloat16
    both = [(0, 1), (1, 0)]

    share = 2 * HD // nx
    slab = rows + 4
    ids = jnp.pad(seg_ids.astype(bf)[None, :], ((0, 31 - rows), (0, 0)))
    chosen = w_keyval[:, (nx - 1) * share :]
    for t in range(nx - 1):
        chosen = jnp.where(it == t, w_keyval[:, t * share : (t + 1) * share], chosen)
    kv_slab = jnp.concatenate([chosen, ids], axis=0)
    folded = jnp.concatenate([kv_slab[i : i + 8] for i in range(0, 32, 8)], axis=1)
    near = spread(folded, ("yh", "z"), ny * nz)

    ring = lambda k: [(i, (i + k) % nx) for i in range(nx)]
    others = [lax.ppermute(tokens, "tp", ring(k)) for k in range(1, nx)]

    qo_near = spread(after(jnp.concatenate([w_query, w_out.T], axis=0), near), ("yh", "z"), ny * nz)
    part = ny * nz * rows
    qo_send = jnp.concatenate(
        [qo_near[:, :rows].reshape(part, cols), qo_near[:, rows:].reshape(part, cols)], axis=0
    )
    qo_all = lax.all_gather(qo_send, ("x", "c"), axis=0, tiled=False)

    kv_near = jnp.concatenate([near[:, :, i * share : (i + 1) * share] for i in range(slab // 8)], axis=1)
    kv_far_x = [lax.ppermute(kv_near, "x", ring(k)) for k in range(1, nx)]
    kv_mine = jnp.stack(in_order([kv_near, *kv_far_x], ix))
    kv_twin = lax.ppermute(kv_mine, "c", both)

    normed = rms_norm(jnp.concatenate(in_order([tokens, *others], it), axis=1), norm_gain)
    padded = turned(normed, natural_to_gathered(shard, rows, slab))
    half = ny * nz * slab
    of_core = [
        jnp.concatenate([padded[:, i * half : (i + 1) * half] for i in range(c, nx * nc, nc)], axis=1)
        for c in range(nc)
    ]
    for_mine = jnp.where(ic == 0, of_core[0], of_core[1])
    for_twin = jnp.where(ic == 0, of_core[1], of_core[0])

    all_ids = jnp.concatenate([kv_mine[:, :, rows], kv_twin[:, :, rows]], axis=0).astype(jnp.int32)
    labels = jnp.arange(SEGS, dtype=jnp.int32)
    starts = jnp.sum((all_ids.reshape(-1)[None, :] < labels[:, None]).astype(jnp.int32), axis=1)
    own_start = jnp.sum(jnp.where(seg_ids[:, None] == labels[None, :], starts[None, :], 0), axis=1)
    token_index = my_index * tok + jnp.arange(tok, dtype=jnp.int32)
    cosine, sine = angles((token_index - own_start).astype(jnp.float32))

    kv_raw = jnp.dot(
        for_mine, kv_mine.reshape(nx * half, share), preferred_element_type=jnp.float32
    ) + jnp.dot(for_twin, kv_twin.reshape(nx * half, share), preferred_element_type=jnp.float32)
    quarter = HD // 4
    swapped = jnp.concatenate([kv_raw[:, quarter:], kv_raw[:, :quarter]], axis=1)
    kv_share = jnp.where(it == 0, kv_raw * cosine + swapped * sine, kv_raw).astype(bf)

    block = nz * nc
    devices = nx * ny * block
    before = lax.ppermute(kv_share, SEQ, [(i, i + block) for i in range(devices - block)])
    chips = jnp.arange(nz, dtype=jnp.int32)
    to_send = jnp.where((chips > iz)[:, None, None], kv_share[None], before[None])
    to_send = after(to_send, qo_send)
    to_send = jnp.broadcast_to(to_send[:, None], (nz, nx, tok, share)).reshape(nz * nx, tok, share)
    mine = lax.all_to_all(to_send, ("z", "tp"), 0, 0, tiled=True).reshape(nz, nx, tok, share)
    rest = [lax.ppermute(kv_share, "tp", [(i, (i + k) % nx) for i in range(nx)]) for k in range(1, nx)]
    own_kv = jnp.stack(in_order([kv_share, *rest], it))
    kv_cache = jnp.concatenate(list(own_kv), axis=1)
    at_self = (chips == iz)[:, None, None, None] & (ic == 0)
    partner = lax.ppermute(jnp.where(at_self, own_kv[None], mine), "c", both)
    perm = natural_to_gathered(shard, rows, rows)
    reordered = turned(after(normed, to_send), perm)
    block_of_mine = my_block - (chips >= iz).astype(jnp.int32)
    block_of_partner = my_block - jnp.where(ic == 1, chips > iz, chips >= iz).astype(jnp.int32)
    first_of_mine = ((block_of_mine * nz + chips) * nc + ic) * tok
    first_of_partner = ((block_of_partner * nz + chips) * nc + 1 - ic) * tok
    firsts = jnp.concatenate([first_of_mine, first_of_partner, my_index[None] * tok])
    keys_at = (firsts[:, None] + jnp.arange(tok, dtype=jnp.int32)[None, :]).reshape(1, -1)

    vmem = pl.BlockSpec(memory_space=pltpu.VMEM)
    hbm = pl.BlockSpec(memory_space=pl.ANY)
    scratch = [pltpu.VMEM((nx * shard, cols), bf), pltpu.SemaphoreType.DMA((nx * nc,))]
    queries = pl.pallas_call(
        queries_kernel,
        out_shape=jax.ShapeDtypeStruct((tok, cols), bf),
        in_specs=[vmem, vmem, vmem, hbm],
        out_specs=vmem,
        scratch_shapes=scratch,
        name="queries",
    )(reordered, cosine, sine, qo_all)
    reach_back = jnp.maximum(own_start, token_index - (WINDOW - 1))
    partial = pl.pallas_call(
        attend_kernel,
        out_shape=jax.ShapeDtypeStruct((nx, tok, shard), bf),
        in_specs=[vmem] * 7 + [hbm],
        out_specs=vmem,
        scratch_shapes=scratch,
        name="attend",
    )(queries, mine, partner, own_kv, keys_at, token_index[:, None], reach_back[:, None], qo_all)

    received = lax.all_to_all(partial, "tp", 0, 0, tiled=True)
    summed = jnp.zeros((tok, shard), jnp.float32)
    for g in range(nx):
        summed = summed + lax.dot_general(
            received[g], perm, (((1,), (1,)), ((), ())), preferred_element_type=jnp.float32
        )
    hidden = (tokens.astype(jnp.float32) + summed).astype(bf)
    return (hidden, kv_cache)


def solution(mesh):
    fine = Mesh(mesh.devices.reshape(*GRID, mesh.shape["tp"]), (*SEQ, "tp"))
    in_specs = (P(SEQ, "tp"), P(SEQ), P(), P(SEQ, "tp"), P(SEQ, None), P("tp", SEQ))
    out_specs = (P(SEQ, "tp"), P(SEQ, None))
    return jax.shard_map(per_device, mesh=fine, in_specs=in_specs, out_specs=out_specs, check_vma=False)
```

```python
import jax
import jax.numpy as jnp
from jax import lax
from jax.experimental import pallas as pl
from jax.experimental.pallas import tpu as pltpu
from jax.sharding import Mesh, PartitionSpec as P


HD = 256
WINDOW = 2048
SEGS = 32
GRID = (4, 2, 8, 2)
SEQ = ("x", "yh", "z", "c")


def rms_norm(values, gain):
    wide = values.astype(jnp.float32)
    scaled = wide * lax.rsqrt(jnp.mean(wide * wide, axis=-1, keepdims=True) + 1e-06)
    return (scaled * gain.astype(jnp.float32)).astype(jnp.bfloat16)


def angles(positions):
    quarter = HD // 4
    freq = 10000.0 ** (-jnp.arange(quarter, dtype=jnp.float32) / quarter)
    angle = positions[:, None] * freq
    cosine, sine = jnp.cos(angle), jnp.sin(angle)
    return jnp.concatenate([cosine, cosine], axis=1), jnp.concatenate([-sine, sine], axis=1)


def after(value, *others):
    return lax.optimization_barrier((value, *others))[0]


def spread(slab, axes, count):
    copies = jnp.broadcast_to(slab[None], (count, *slab.shape))
    return lax.all_to_all(copies, axes, 0, 0, tiled=True)


def in_order(shares, here):
    count = len(shares)
    ordered = []
    for g in range(count):
        came = (here - g) % count
        share = shares[count - 1]
        for k in range(count - 1):
            share = jnp.where(came == k, shares[k], share)
        ordered.append(share)
    return ordered


def natural_to_gathered(per, rows, slab):
    width = per // rows * slab
    nat = lax.broadcasted_iota(jnp.int32, (per, width), 0)
    gat = lax.broadcasted_iota(jnp.int32, (per, width), 1)
    half = width // 2
    core, rest = gat // half, gat % half
    place, row = rest // slab, rest % slab
    source = (place * 2 + core) * rows + row
    return ((nat == source) & (row < rows)).astype(jnp.bfloat16)


def turned(values, hot):
    per = hot.shape[0]
    return jnp.concatenate(
        [
            jnp.dot(values[:, g : g + per], hot, preferred_element_type=jnp.float32).astype(jnp.bfloat16)
            for g in range(0, values.shape[1], per)
        ],
        axis=1,
    )


def fetch(qo_ref, at, weights_ref, sems):
    groups = qo_ref.shape[0]
    part = qo_ref.shape[1] // 2
    copies = [
        pltpu.make_async_copy(
            qo_ref.at[g, pl.ds(at * part, part), :], weights_ref.at[pl.ds(g * part, part), :], sems.at[g]
        )
        for g in range(groups)
    ]
    for copy in copies:
        copy.start()
    return copies


def queries_kernel(normed_ref, cosine_ref, sine_ref, qo_ref, out_ref, weights_ref, sems):
    for copy in fetch(qo_ref, 0, weights_ref, sems):
        copy.wait()
    raw = jnp.dot(normed_ref[...], weights_ref[...], preferred_element_type=jnp.float32) * HD ** (-0.5)
    half = HD // 2
    for h in range(raw.shape[1] // HD):
        lo = raw[:, h * HD : h * HD + half]
        turned = lo * cosine_ref[...] + pltpu.roll(lo, half // 2, 1) * sine_ref[...]
        out_ref[:, h * HD : h * HD + half] = turned.astype(out_ref.dtype)
        out_ref[:, h * HD + half : (h + 1) * HD] = raw[:, h * HD + half : (h + 1) * HD].astype(
            out_ref.dtype
        )


def scores_of(queries_ref, h, keys, live):
    scores = lax.dot_general(
        queries_ref[:, h * HD : (h + 1) * HD], keys, (((1,), (1,)), ((), ())), preferred_element_type=jnp.float32
    )
    return jnp.where(live, scores, -1e30)


def near_kernel(queries_ref, mine_ref, own_ref, keys_at_ref, token_ref, first_ref, sums_ref, stats_ref):
    def whole(t):
        far = mine_ref[:, t].reshape(mine_ref.shape[0] * mine_ref.shape[2], mine_ref.shape[3])
        return jnp.concatenate([far, own_ref[t]], axis=0)

    keys = jnp.concatenate([whole(0), whole(1)], axis=1)
    values = jnp.concatenate([whole(2), whole(3)], axis=1)
    at = keys_at_ref[...]
    live = (at <= token_ref[...]) & (at >= first_ref[...])
    heads = queries_ref.shape[1] // HD
    for h in range(heads):
        scores = scores_of(queries_ref, h, keys, live)
        peak = jnp.max(scores, axis=1, keepdims=True)
        powered = jnp.exp(scores - peak)
        stats_ref[h] = jnp.broadcast_to(peak, stats_ref.shape[1:])
        stats_ref[heads + h] = jnp.broadcast_to(
            jnp.sum(powered, axis=1, keepdims=True), stats_ref.shape[1:]
        )
        sums_ref[:, h * HD : (h + 1) * HD] = jnp.dot(
            powered.astype(jnp.bfloat16), values, preferred_element_type=jnp.float32
        )


def attend_kernel(
    queries_ref, partner_ref, keys_at_ref, token_ref, first_ref, sums_ref, stats_ref, qo_ref, out_ref, weights_ref, sems
):
    copies = fetch(qo_ref, 1, weights_ref, sems)
    whole = lambda t: partner_ref[:, t].reshape(
        partner_ref.shape[0] * partner_ref.shape[2], partner_ref.shape[3]
    )
    keys = jnp.concatenate([whole(0), whole(1)], axis=1)
    values = jnp.concatenate([whole(2), whole(3)], axis=1)
    at = keys_at_ref[...]
    live = (at <= token_ref[...]) & (at >= first_ref[...])
    heads = []
    count = queries_ref.shape[1] // HD
    for h in range(count):
        scores = scores_of(queries_ref, h, keys, live)
        before = stats_ref[h][:, :1]
        peak = jnp.maximum(before, jnp.max(scores, axis=1, keepdims=True))
        powered = jnp.exp(scores - peak)
        shrink = jnp.exp(before - peak)
        total = shrink * stats_ref[count + h][:, :1] + jnp.sum(powered, axis=1, keepdims=True)
        summed = shrink * sums_ref[:, h * HD : (h + 1) * HD] + jnp.dot(
            powered.astype(jnp.bfloat16), values, preferred_element_type=jnp.float32
        )
        heads.append((summed * (1.0 / total)).astype(jnp.bfloat16))
    attended = jnp.concatenate(heads, axis=1)
    shard = out_ref.shape[2]
    for copy in copies:
        copy.wait()
    for g in range(out_ref.shape[0]):
        out_ref[g] = lax.dot_general(
            attended,
            weights_ref[g * shard : (g + 1) * shard, :],
            (((1,), (1,)), ((), ())),
            preferred_element_type=jnp.float32,
        ).astype(out_ref.dtype)


def per_device(tokens, seg_ids, norm_gain, w_query, w_keyval, w_out):
    nx, ny, nz, nc = GRID
    tok, shard = tokens.shape
    rows = w_query.shape[0]
    cols = w_query.shape[1]
    ix, iy, iz, ic = (lax.axis_index(a) for a in SEQ)
    it = lax.axis_index("tp")
    my_block = ix * ny + iy
    my_index = (my_block * nz + iz) * nc + ic
    bf = jnp.bfloat16
    both = [(0, 1), (1, 0)]

    share = 2 * HD // nx
    slab = rows + 4
    ids = jnp.pad(seg_ids.astype(bf)[None, :], ((0, 31 - rows), (0, 0)))
    chosen = w_keyval[:, (nx - 1) * share :]
    for t in range(nx - 1):
        chosen = jnp.where(it == t, w_keyval[:, t * share : (t + 1) * share], chosen)
    kv_slab = jnp.concatenate([chosen, ids], axis=0)
    folded = jnp.concatenate([kv_slab[i : i + 8] for i in range(0, 32, 8)], axis=1)
    near = spread(jnp.concatenate([w_query, w_out.T, folded], axis=0), ("yh", "z"), ny * nz)

    others = [lax.ppermute(tokens, "tp", [(i, (i + k) % nx) for i in range(nx)]) for k in range(1, nx)]

    kv_near = jnp.concatenate(
        [near[:, 2 * rows :, i * share : (i + 1) * share] for i in range(slab // 8)], axis=1
    )
    kv_mine = spread(kv_near, "x", nx)
    kv_twin = lax.ppermute(kv_mine, "c", both)
    part = nz * ny * rows
    qo_send = jnp.concatenate(
        [near[:, :rows].reshape(part, cols), near[:, rows : 2 * rows].reshape(part, cols)], axis=0
    )
    qo_all = lax.all_gather(qo_send, ("x", "c"), axis=0, tiled=False)

    *others, _ = lax.optimization_barrier((*others, qo_send))
    normed = rms_norm(jnp.concatenate(in_order([tokens, *others], it), axis=1), norm_gain)
    padded = turned(normed, natural_to_gathered(shard, rows, slab))
    half = ny * nz * slab
    of_core = [
        jnp.concatenate([padded[:, i * half : (i + 1) * half] for i in range(c, nx * nc, nc)], axis=1)
        for c in range(nc)
    ]
    for_mine = jnp.where(ic == 0, of_core[0], of_core[1])
    for_twin = jnp.where(ic == 0, of_core[1], of_core[0])
    kv_mine, for_mine, for_twin = lax.optimization_barrier((kv_mine, for_mine, for_twin))

    all_ids = jnp.concatenate([kv_mine[:, :, rows], kv_twin[:, :, rows]], axis=0).astype(jnp.int32)
    labels = jnp.arange(SEGS, dtype=jnp.int32)
    starts = jnp.sum((all_ids.reshape(-1)[None, :] < labels[:, None]).astype(jnp.int32), axis=1)
    own_start = jnp.sum(jnp.where(seg_ids[:, None] == labels[None, :], starts[None, :], 0), axis=1)
    token_index = my_index * tok + jnp.arange(tok, dtype=jnp.int32)
    cosine, sine = angles((token_index - own_start).astype(jnp.float32))

    kv_raw = jnp.dot(
        for_mine, kv_mine.reshape(nx * half, share), preferred_element_type=jnp.float32
    ) + jnp.dot(for_twin, kv_twin.reshape(nx * half, share), preferred_element_type=jnp.float32)
    quarter = HD // 4
    swapped = jnp.concatenate([kv_raw[:, quarter:], kv_raw[:, :quarter]], axis=1)
    kv_share = jnp.where(it == 0, kv_raw * cosine + swapped * sine, kv_raw).astype(bf)

    block = nz * nc
    devices = nx * ny * block
    before = lax.ppermute(kv_share, SEQ, [(i, i + block) for i in range(devices - block)])
    chips = jnp.arange(nz, dtype=jnp.int32)
    to_send = jnp.where((chips > iz)[:, None, None], kv_share[None], before[None])
    to_send = jnp.broadcast_to(to_send[:, None], (nz, nx, tok, share)).reshape(nz * nx, tok, share)
    mine = lax.all_to_all(to_send, ("z", "tp"), 0, 0, tiled=True).reshape(nz, nx, tok, share)
    rest = [lax.ppermute(kv_share, "tp", [(i, (i + k) % nx) for i in range(nx)]) for k in range(1, nx)]
    own_kv = jnp.stack(in_order([kv_share, *rest], it))
    kv_cache = jnp.concatenate(list(own_kv), axis=1)
    at_self = (chips == iz)[:, None, None, None] & (ic == 0)
    partner = lax.ppermute(jnp.where(at_self, own_kv[None], mine), "c", both)
    perm = natural_to_gathered(shard, rows, rows)
    reordered = turned(after(normed, to_send), perm)
    block_of_mine = my_block - (chips >= iz).astype(jnp.int32)
    block_of_partner = my_block - jnp.where(ic == 1, chips > iz, chips >= iz).astype(jnp.int32)
    first_of_mine = ((block_of_mine * nz + chips) * nc + ic) * tok
    first_of_partner = ((block_of_partner * nz + chips) * nc + 1 - ic) * tok
    along = jnp.arange(tok, dtype=jnp.int32)[None, :]
    near_firsts = jnp.concatenate([first_of_mine, my_index[None] * tok])
    near_at = (near_firsts[:, None] + along).reshape(1, -1)
    far_at = (first_of_partner[:, None] + along).reshape(1, -1)

    vmem = pl.BlockSpec(memory_space=pltpu.VMEM)
    hbm = pl.BlockSpec(memory_space=pl.ANY)
    scratch = [pltpu.VMEM((nx * nc * part, cols), bf), pltpu.SemaphoreType.DMA((nx * nc,))]
    queries = pl.pallas_call(
        queries_kernel,
        out_shape=jax.ShapeDtypeStruct((tok, cols), bf),
        in_specs=[vmem, vmem, vmem, hbm],
        out_specs=vmem,
        scratch_shapes=scratch,
        name="queries",
    )(reordered, cosine, sine, qo_all)
    reach_back = jnp.maximum(own_start, token_index - (WINDOW - 1))
    token_at, first_at = token_index[:, None], reach_back[:, None]
    heads = cols // HD
    sums, stats = pl.pallas_call(
        near_kernel,
        out_shape=(
            jax.ShapeDtypeStruct((tok, cols), jnp.float32),
            jax.ShapeDtypeStruct((2 * heads, tok, share), jnp.float32),
        ),
        in_specs=[vmem] * 6,
        out_specs=(vmem, vmem),
        name="near",
    )(queries, mine, own_kv, near_at, token_at, first_at)
    partial = pl.pallas_call(
        attend_kernel,
        out_shape=jax.ShapeDtypeStruct((nx, tok, shard), bf),
        in_specs=[vmem] * 7 + [hbm],
        out_specs=vmem,
        scratch_shapes=scratch,
        name="attend",
    )(queries, partner, far_at, token_at, first_at, sums, stats, qo_all)

    received = lax.all_to_all(partial, "tp", 0, 0, tiled=True)
    summed = jnp.zeros((tok, shard), jnp.float32)
    for g in range(nx):
        summed = summed + lax.dot_general(
            received[g], perm, (((1,), (1,)), ((), ())), preferred_element_type=jnp.float32
        )
    hidden = (tokens.astype(jnp.float32) + summed).astype(bf)
    return (hidden, kv_cache)


def solution(mesh):
    fine = Mesh(mesh.devices.reshape(*GRID, mesh.shape["tp"]), (*SEQ, "tp"))
    in_specs = (P(SEQ, "tp"), P(SEQ), P(), P(SEQ, "tp"), P(SEQ, None), P("tp", SEQ))
    out_specs = (P(SEQ, "tp"), P(SEQ, None))
    return jax.shard_map(per_device, mesh=fine, in_specs=in_specs, out_specs=out_specs, check_vma=False)
```

```python
import jax
import jax.numpy as jnp
from jax import lax
from jax.experimental import pallas as pl
from jax.experimental.pallas import tpu as pltpu
from jax.sharding import Mesh, PartitionSpec as P


HD = 256
WINDOW = 2048
SEGS = 32
GRID = (4, 2, 8, 2)
SEQ = ("x", "yh", "z", "c")


def rms_norm(values, gain):
    wide = values.astype(jnp.float32)
    scaled = wide * lax.rsqrt(jnp.mean(wide * wide, axis=-1, keepdims=True) + 1e-06)
    return (scaled * gain.astype(jnp.float32)).astype(jnp.bfloat16)


def angles(positions):
    quarter = HD // 4
    freq = 10000.0 ** (-jnp.arange(quarter, dtype=jnp.float32) / quarter)
    angle = positions[:, None] * freq
    cosine, sine = jnp.cos(angle), jnp.sin(angle)
    return jnp.concatenate([cosine, cosine], axis=1), jnp.concatenate([-sine, sine], axis=1)


def after(value, *others):
    return lax.optimization_barrier((value, *others))[0]


def spread(slab, axes, count):
    copies = jnp.broadcast_to(slab[None], (count, *slab.shape))
    return lax.all_to_all(copies, axes, 0, 0, tiled=True)


def in_order(shares, here):
    count = len(shares)
    ordered = []
    for g in range(count):
        came = (here - g) % count
        share = shares[count - 1]
        for k in range(count - 1):
            share = jnp.where(came == k, shares[k], share)
        ordered.append(share)
    return ordered


def natural_to_gathered(per, rows, slab):
    width = per // rows * slab
    nat = lax.broadcasted_iota(jnp.int32, (per, width), 0)
    gat = lax.broadcasted_iota(jnp.int32, (per, width), 1)
    half = width // 2
    core, rest = gat // half, gat % half
    place, row = rest // slab, rest % slab
    source = (place * 2 + core) * rows + row
    return ((nat == source) & (row < rows)).astype(jnp.bfloat16)


def turned(values, hot):
    per = hot.shape[0]
    return jnp.concatenate(
        [
            jnp.dot(values[:, g : g + per], hot, preferred_element_type=jnp.float32).astype(jnp.bfloat16)
            for g in range(0, values.shape[1], per)
        ],
        axis=1,
    )


def on_core(value):
    return pltpu.with_memory_space_constraint(value, pltpu.VMEM)


def fetch(qo_ref, at, weights_ref, sems):
    groups = qo_ref.shape[0]
    part = qo_ref.shape[1] // 2
    copies = [
        pltpu.make_async_copy(
            qo_ref.at[g, pl.ds(at * part, part), :], weights_ref.at[pl.ds(g * part, part), :], sems.at[g]
        )
        for g in range(groups)
    ]
    for copy in copies:
        copy.start()
    return copies


def queries_kernel(normed_ref, cosine_ref, sine_ref, qo_ref, out_ref, weights_ref, sems):
    for copy in fetch(qo_ref, 0, weights_ref, sems):
        copy.wait()
    raw = jnp.dot(normed_ref[...], weights_ref[...], preferred_element_type=jnp.float32) * HD ** (-0.5)
    half = HD // 2
    for h in range(raw.shape[1] // HD):
        lo = raw[:, h * HD : h * HD + half]
        turned = lo * cosine_ref[...] + pltpu.roll(lo, half // 2, 1) * sine_ref[...]
        out_ref[:, h * HD : h * HD + half] = turned.astype(out_ref.dtype)
        out_ref[:, h * HD + half : (h + 1) * HD] = raw[:, h * HD + half : (h + 1) * HD].astype(
            out_ref.dtype
        )


def attend_kernel(
    queries_ref, mine_ref, partner_ref, own_ref, keys_at_ref, token_ref, first_ref, qo_ref, out_ref, weights_ref, sems
):
    copies = fetch(qo_ref, 1, weights_ref, sems)

    def whole(t):
        far = [ref[:, t].reshape(ref.shape[0] * ref.shape[2], ref.shape[3]) for ref in (mine_ref, partner_ref)]
        return jnp.concatenate([*far, own_ref[t]], axis=0)

    keys = jnp.concatenate([whole(0), whole(1)], axis=1)
    values = jnp.concatenate([whole(2), whole(3)], axis=1)
    at = keys_at_ref[...]
    live = (at <= token_ref[...]) & (at >= first_ref[...])
    heads = []
    for h in range(queries_ref.shape[1] // HD):
        scores = lax.dot_general(
            queries_ref[:, h * HD : (h + 1) * HD],
            keys,
            (((1,), (1,)), ((), ())),
            preferred_element_type=jnp.float32,
        )
        scores = jnp.where(live, scores, -1e30)
        powered = jnp.exp(scores - jnp.max(scores, axis=1, keepdims=True))
        weights = (powered * (1.0 / jnp.sum(powered, axis=1, keepdims=True))).astype(jnp.bfloat16)
        heads.append(
            jnp.dot(weights, values, preferred_element_type=jnp.float32).astype(jnp.bfloat16)
        )
    attended = jnp.concatenate(heads, axis=1)
    shard = out_ref.shape[2]
    for copy in copies:
        copy.wait()
    for g in range(out_ref.shape[0]):
        out_ref[g] = lax.dot_general(
            attended,
            weights_ref[g * shard : (g + 1) * shard, :],
            (((1,), (1,)), ((), ())),
            preferred_element_type=jnp.float32,
        ).astype(out_ref.dtype)


def per_device(tokens, seg_ids, norm_gain, w_query, w_keyval, w_out):
    nx, ny, nz, nc = GRID
    tok, shard = tokens.shape
    rows = w_query.shape[0]
    cols = w_query.shape[1]
    ix, iy, iz, ic = (lax.axis_index(a) for a in SEQ)
    it = lax.axis_index("tp")
    my_block = ix * ny + iy
    my_index = (my_block * nz + iz) * nc + ic
    bf = jnp.bfloat16
    both = [(0, 1), (1, 0)]

    share = 2 * HD // nx
    slab = rows + 4
    ids = jnp.pad(seg_ids.astype(bf)[None, :], ((0, 31 - rows), (0, 0)))
    chosen = w_keyval[:, (nx - 1) * share :]
    for t in range(nx - 1):
        chosen = jnp.where(it == t, w_keyval[:, t * share : (t + 1) * share], chosen)
    kv_slab = jnp.concatenate([chosen, ids], axis=0)
    folded = jnp.concatenate([kv_slab[i : i + 8] for i in range(0, 32, 8)], axis=1)
    near = spread(jnp.concatenate([w_query, w_out.T, folded], axis=0), ("yh", "z"), ny * nz)

    others = [lax.ppermute(tokens, "tp", [(i, (i + k) % nx) for i in range(nx)]) for k in range(1, nx)]

    kv_near = jnp.concatenate(
        [near[:, 2 * rows :, i * share : (i + 1) * share] for i in range(slab // 8)], axis=1
    )
    kv_all = spread(kv_near, ("x", "c"), nx * nc)
    part = nz * ny * rows
    qo_send = jnp.concatenate(
        [near[:, :rows].reshape(part, cols), near[:, rows : 2 * rows].reshape(part, cols)], axis=0
    )
    qo_all = lax.all_gather(qo_send, ("x", "c"), axis=0, tiled=False)

    groups = in_order([tokens, *others], it)
    normed = rms_norm(jnp.concatenate(groups, axis=1), norm_gain)
    padded = turned(normed, natural_to_gathered(shard, rows, slab))
    kv_all, padded = lax.optimization_barrier((kv_all, padded))

    all_ids = kv_all[:, :, rows].astype(jnp.int32)
    labels = jnp.arange(SEGS, dtype=jnp.int32)
    starts = jnp.sum((all_ids.reshape(-1)[None, :] < labels[:, None]).astype(jnp.int32), axis=1)
    own_start = jnp.sum(jnp.where(seg_ids[:, None] == labels[None, :], starts[None, :], 0), axis=1)
    token_index = my_index * tok + jnp.arange(tok, dtype=jnp.int32)
    cosine, sine = angles((token_index - own_start).astype(jnp.float32))

    kv_raw = jnp.dot(
        padded, kv_all.reshape(nx * nc * ny * nz * slab, share), preferred_element_type=jnp.float32
    )
    quarter = HD // 4
    swapped = jnp.concatenate([kv_raw[:, quarter:], kv_raw[:, :quarter]], axis=1)
    kv_share = jnp.where(it == 0, kv_raw * cosine + swapped * sine, kv_raw).astype(bf)

    block = nz * nc
    devices = nx * ny * block
    before = lax.ppermute(kv_share, SEQ, [(i, i + block) for i in range(devices - block)])
    chips = jnp.arange(nz, dtype=jnp.int32)
    to_send = jnp.where((chips > iz)[:, None, None], kv_share[None], before[None])
    to_send = jnp.broadcast_to(to_send[:, None], (nz, nx, tok, share)).reshape(nz * nx, tok, share)
    mine = lax.all_to_all(to_send, ("z", "tp"), 0, 0, tiled=True).reshape(nz, nx, tok, share)
    rest = [lax.ppermute(kv_share, "tp", [(i, (i + k) % nx) for i in range(nx)]) for k in range(1, nx)]
    own_kv = jnp.stack(in_order([kv_share, *rest], it))
    kv_cache = jnp.concatenate(list(own_kv), axis=1)
    at_self = (chips == iz)[:, None, None, None] & (ic == 0)
    partner = lax.ppermute(jnp.where(at_self, own_kv[None], mine), "c", both)
    perm = natural_to_gathered(shard, rows, rows)
    reordered = turned(after(normed, to_send), perm)
    block_of_mine = my_block - (chips >= iz).astype(jnp.int32)
    block_of_partner = my_block - jnp.where(ic == 1, chips > iz, chips >= iz).astype(jnp.int32)
    first_of_mine = ((block_of_mine * nz + chips) * nc + ic) * tok
    first_of_partner = ((block_of_partner * nz + chips) * nc + 1 - ic) * tok
    firsts = jnp.concatenate([first_of_mine, first_of_partner, my_index[None] * tok])
    keys_at = (firsts[:, None] + jnp.arange(tok, dtype=jnp.int32)[None, :]).reshape(1, -1)

    vmem = pl.BlockSpec(memory_space=pltpu.VMEM)
    hbm = pl.BlockSpec(memory_space=pl.ANY)
    scratch = [pltpu.VMEM((nx * nc * part, cols), bf), pltpu.SemaphoreType.DMA((nx * nc,))]
    queries = pl.pallas_call(
        queries_kernel,
        out_shape=jax.ShapeDtypeStruct((tok, cols), bf),
        in_specs=[vmem, vmem, vmem, hbm],
        out_specs=vmem,
        scratch_shapes=scratch,
        name="queries",
    )(*(on_core(a) for a in (reordered, cosine, sine)), qo_all)
    reach_back = jnp.maximum(own_start, token_index - (WINDOW - 1))
    partial = pl.pallas_call(
        attend_kernel,
        out_shape=jax.ShapeDtypeStruct((nx, tok, shard), bf),
        in_specs=[vmem] * 7 + [hbm],
        out_specs=vmem,
        scratch_shapes=scratch,
        name="attend",
    )(
        *(on_core(a) for a in (queries, mine, partner, own_kv, keys_at, token_index[:, None], reach_back[:, None])),
        qo_all,
    )

    received = lax.all_to_all(partial, "tp", 0, 0, tiled=True)
    summed = jnp.zeros((tok, shard), jnp.float32)
    for g in range(nx):
        summed = summed + lax.dot_general(
            received[g], perm, (((1,), (1,)), ((), ())), preferred_element_type=jnp.float32
        )
    hidden = (tokens.astype(jnp.float32) + summed).astype(bf)
    return (hidden, kv_cache)


def solution(mesh):
    fine = Mesh(mesh.devices.reshape(*GRID, mesh.shape["tp"]), (*SEQ, "tp"))
    in_specs = (P(SEQ, "tp"), P(SEQ), P(), P(SEQ, "tp"), P(SEQ, None), P("tp", SEQ))
    out_specs = (P(SEQ, "tp"), P(SEQ, None))
    return jax.shard_map(per_device, mesh=fine, in_specs=in_specs, out_specs=out_specs, check_vma=False)
```
